512 devices in a mesh: ctx: 64 (over x, z), head: 8 (over y, core).
Axes of the slice: x: 4, y: 4, z: 16, core: 2. Of those that a mesh axis runs over, the one named last changes fastest.
Arguments:
- hidden_in: bfloat16 [65536, 2048], P('ctx', 'head'), may hold values from -6 to 6
- proj_weight: bfloat16 [2048, 3584], P(None, 'head'), may hold values from -0.125 to 0.125
- conv_weight: float32 [3, 1024], P(None, 'head'), may hold values from -3 to 3
- norm_gain: float32 [1024], P('head'), may hold values from 0.1 to 1.9
- out_weight: bfloat16 [1024, 2048], P('head'), may hold values from -0.25 to 0.25
Outputs:
- layer_out: bfloat16 [65536, 2048], P('ctx', 'head')
The draws below stay inside these ranges and needn't reach their ends.
All inputs are finite; a program needn't handle non-finite values.
Results may differ from the reference program's by a relative error of at most 0.014.
Values may be sent and summed in bfloat16 or wider, within the bound.
A program may use at most 64 MiB of HBM per device.

```python
import jax
import jax.numpy as jnp
from jax import lax

D = 2048
HEADS = 16
DV = 64
FQK = 16
WIN = 64
CONV = 3
TOK_DEV = 1024
TOKENS = 65536
N_HEAD = 8


def with_spikes(values, key, source, target, parts, factor):
    def block_of(axis_at):
        return (jnp.arange(values.shape[axis_at]) // (values.shape[axis_at] // parts)).reshape((-1,) + (1,) * (values.ndim - 1 - axis_at))

    first = jax.random.permutation(key, parts)[block_of(target)]
    far = (block_of(target) + parts // 2) % parts
    return jnp.where((block_of(source) == first) | (block_of(source) == far), factor * values, values)


def level_of(own_key, dims, split, least, high):
    factor_of, own = 1.0, jax.random.fold_in(own_key, 6)
    for dim, parts in split:
        draws = jnp.exp(jax.random.uniform(jax.random.fold_in(own, dim), (parts,), jnp.float32, least / len(split), high / len(split)))
        factor_of = factor_of * jnp.repeat(draws, dims[dim] // parts).reshape([-1 if axis == dim else 1 for axis in range(len(dims))])
    return factor_of


def gaussian(own_key, shape, spread, most, cuts=(), held_as=jnp.bfloat16):
    entries = spread * jax.random.normal(own_key, shape, jnp.float32)
    if cuts:
        entries = entries * level_of(own_key, shape, cuts, -0.22, 0.18)
    return jnp.clip(entries, -most, most).astype(held_as)


def noise_with(stream_key, extent, width, most, split, heavy, kind=jnp.bfloat16):
    result = width * jax.random.normal(stream_key, extent, jnp.float32)
    if split:
        result = result * level_of(stream_key, extent, split, -0.22, 0.18)
    return jnp.clip(with_spikes(result, jax.random.fold_in(stream_key, 3), *heavy), -most, most).astype(kind)


def setup_inputs(seed: int = 0) -> dict:
    seeds = jax.random.split(jax.random.key(seed), 6)
    return {
        "hidden_in": gaussian(seeds[0], (TOKENS, D), 1.0, 6.0, ((0, 64), (1, 8))),
        "proj_weight": gaussian(seeds[1], (D, HEADS * (2 * FQK + 3 * DV)), D ** -0.5, 0.125, ((1, 8),)),
        "conv_weight": gaussian(seeds[2], (CONV, HEADS * DV), 0.6, 3.0, ((1, 8),), jnp.float32),
        "norm_gain": jnp.clip(1.0 + 0.18 * jax.random.normal(seeds[3], (HEADS * DV,), jnp.float32), 0.1, 1.9),
        "out_weight": noise_with(seeds[4], (HEADS * DV, D), (HEADS * DV) ** -0.5, 0.25, ((0, 8),), (0, 1, 8, 2.0)),
    }


def features(vector):
    vec_len = vector.shape[-1]
    square = (vector[..., :, None] * vector[..., None, :]).reshape(vector.shape[:-1] + (vec_len * vec_len,))
    constant = jnp.ones(vector.shape[:-1] + (1,), vector.dtype)
    return jnp.concatenate([constant, vector / vec_len ** 0.25, square / (2.0 * vec_len) ** 0.5], axis=-1)

def normalize(block_in):
    values = block_in.astype(jnp.float32)
    return (values * lax.rsqrt(lax.optimization_barrier(jnp.mean(values * values, axis=-1, keepdims=True)) + 1e-06)).astype(jnp.bfloat16)

def convolve(extended, conv_weight, count):
    tap_count = conv_weight.shape[0]
    total = jnp.zeros((count, extended.shape[1]), jnp.float32)
    for tap_id in range(tap_count):
        offset = tap_count - 1 - tap_id
        total = total + conv_weight[tap_id] * extended[offset:offset + count].astype(jnp.float32)
    return total.astype(jnp.bfloat16)

def reference(hidden_in, proj_weight, conv_weight, norm_gain, out_weight):
    highest = lax.Precision.HIGHEST
    per_head = 2 * FQK + 3 * DV
    reach_rows = WIN - 1
    projected = jnp.dot(hidden_in, proj_weight, preferred_element_type=jnp.float32).astype(jnp.bfloat16)
    projected = projected.reshape(TOKENS, HEADS, per_head)
    lin_query = projected[:, :, :FQK]
    lin_key = projected[:, :, FQK:2 * FQK]
    raw_values = projected[:, :, 2 * FQK:2 * FQK + DV].reshape(TOKENS, HEADS * DV)
    win_query = projected[:, :, 2 * FQK + DV:2 * FQK + 2 * DV]
    win_key = projected[:, :, 2 * FQK + 2 * DV:]
    padded_raw = jnp.concatenate([jnp.zeros((CONV - 1, HEADS * DV), jnp.bfloat16), raw_values], 0)
    conv_values = convolve(padded_raw, conv_weight, TOKENS).reshape(TOKENS, HEADS, DV)
    q_hat = normalize(win_query)
    k_hat = normalize(win_key)
    pad_keys = jnp.concatenate([jnp.zeros((reach_rows, HEADS, DV), jnp.bfloat16), k_hat], 0)
    pad_values = jnp.concatenate([jnp.zeros((reach_rows, HEADS, DV), jnp.bfloat16), conv_values], 0)
    block_count = TOKENS // TOK_DEV
    causal = jnp.arange(TOK_DEV)[None, :] <= jnp.arange(TOK_DEV)[:, None]
    shift_ids = jnp.arange(TOK_DEV + reach_rows)[None, :] - jnp.arange(TOK_DEV)[:, None]
    band = (shift_ids >= 0) & (shift_ids <= reach_rows)
    gain_grid = norm_gain.reshape(HEADS, DV)

    def split_rows(array):
        return array.reshape((block_count, TOK_DEV) + array.shape[1:])

    def step(prior, inputs):
        query_blk, key_blk, value_blk, qhat_blk, block_id = inputs
        offset = block_id * TOK_DEV
        query_feat = features(query_blk.astype(jnp.float32))
        key_feat = features(key_blk.astype(jnp.float32))
        value_full = value_blk.astype(jnp.float32)
        carried = jnp.einsum('thf,hfd->thd', query_feat, prior, precision=highest)
        products = jnp.einsum('thf,shf->hts', query_blk.astype(jnp.float32), key_blk.astype(jnp.float32), precision=highest)
        scaled = products / FQK ** 0.5
        kernel = jnp.where(causal[None], 1.0 + scaled + 0.5 * scaled * scaled, 0.0).astype(jnp.bfloat16)
        own_part = jnp.einsum('hts,shd->thd', kernel.astype(jnp.float32), value_full, precision=highest)
        lin = carried + own_part
        new_prior = prior + jnp.einsum('thf,thd->hfd', key_feat, value_full, precision=highest)
        keys = lax.dynamic_slice_in_dim(pad_keys, offset, TOK_DEV + reach_rows, 0)
        key_values = lax.dynamic_slice_in_dim(pad_values, offset, TOK_DEV + reach_rows, 0)
        scores = jnp.einsum('thd,shd->hts', qhat_blk.astype(jnp.float32), keys.astype(jnp.float32), precision=highest) / DV ** 0.5
        position = offset + jnp.arange(TOK_DEV + reach_rows).astype(jnp.int32) - reach_rows
        allowed = band & (position >= 0)[None, :]
        expo = jnp.where(allowed[None], jnp.exp(scores), 0.0)
        weights = (expo / lax.optimization_barrier(jnp.sum(expo, axis=-1, keepdims=True))).astype(jnp.bfloat16)
        window = jnp.einsum('hts,shd->thd', weights.astype(jnp.float32), key_values.astype(jnp.float32), precision=highest)
        mean_sq = lax.optimization_barrier(jnp.mean(lin * lin, axis=-1, keepdims=True))
        mixed_heads = (lin * lax.rsqrt(mean_sq + 1e-05) * gain_grid + window).astype(jnp.bfloat16)
        return (new_prior, mixed_heads.reshape(TOK_DEV, HEADS * DV))
    block_ids = jnp.arange(block_count).astype(jnp.int32)
    start_state = jnp.zeros((HEADS, 1 + FQK + FQK * FQK, DV), jnp.float32)
    final_state, mixed = lax.scan(step, start_state, (split_rows(lin_query), split_rows(lin_key), split_rows(conv_values), split_rows(q_hat), block_ids))
    mixed = mixed.reshape(TOKENS, HEADS * DV)
    group_rows = HEADS * DV // N_HEAD
    total = jnp.zeros((TOKENS, D), jnp.float32)
    for group in range(N_HEAD):
        part_sum = jnp.dot(mixed[:, group * group_rows:(group + 1) * group_rows], out_weight[group * group_rows:(group + 1) * group_rows], preferred_element_type=jnp.float32)
        rounded = lax.optimization_barrier(part_sum.astype(jnp.bfloat16))
        total = total + rounded.astype(jnp.float32)
    return total.astype(jnp.bfloat16)
```

```python
import functools

import jax
import jax.numpy as jnp
import numpy as np
from jax import lax
from jax.experimental import pallas as pl
from jax.experimental.pallas import tpu as pltpu
from jax.sharding import PartitionSpec as P

DV = 64
FQK = 16
WIN = 64
CONV = 3
NZ = 16
HALO = 80
FEAT = 160
MESH = pl.DeviceIdType.MESH
F32 = jnp.float32
BF16 = jnp.bfloat16
NT = (((1,), (1,)), ((), ()))


def feature_tables():
    first = np.zeros((FEAT, FQK), np.float32)
    second = np.zeros((FEAT, FQK), np.float32)
    coef = np.zeros((3, FEAT), np.float32)
    row = 0
    for i in range(FQK):
        for j in range(i, FQK):
            first[row, i] = 1.0
            second[row, j] = 1.0
            coef[0, row] = (1.0 if i == j else 2.0**0.5) / (2.0 * FQK) ** 0.5
            row += 1
    for i in range(FQK):
        first[row, i] = 1.0
        coef[0, row] = 1.0 / FQK**0.25
        coef[1, row] = 1.0
        row += 1
    coef[2, row] = 1.0
    return np.stack([first, second]), coef


def dot(a, b):
    return jnp.dot(a, b, preferred_element_type=F32)


def dot_nt(a, b):
    return lax.dot_general(a, b, NT, preferred_element_type=F32)


def gather_matmul_kernel(x_ref, w_hbm, o_ref, buf, wv, acc, wsem, ssem, rsem):
    ctx = lax.axis_index("ctx")
    me = lax.axis_index("head")
    rows, depth = x_ref.shape
    half = rows // 2
    y = lax.div(me, 2)
    core = lax.rem(me, 2)
    other = 1 - core
    y_left, y_right, y_far = lax.rem(y + 3, 4), lax.rem(y + 1, 4), lax.rem(y + 2, 4)
    left, right = y_left * 2 + core, y_right * 2 + core
    partner = y * 2 + other
    owners = [
        left,
        right,
        y_far * 2 + core,
        partner,
        y_left * 2 + other,
        y_right * 2 + other,
        y_far * 2 + other,
    ]

    w_copy = pltpu.make_async_copy(w_hbm, wv, wsem)
    w_copy.start()
    barrier = pltpu.get_barrier_semaphore()
    for dev in (left, right, partner):
        pl.semaphore_signal(barrier, inc=1, device_id=(ctx, dev), device_id_type=MESH)
    pl.semaphore_wait(barrier, 3)

    sent = []

    def send(src, slot, part, dev):
        span = pl.ds(part * half, half)
        copy = pltpu.make_async_remote_copy(
            src_ref=src.at[span],
            dst_ref=buf.at[slot, span],
            send_sem=ssem.at[len(sent)],
            recv_sem=rsem.at[slot * 2 + part],
            device_id=(ctx, dev),
            device_id_type=MESH,
        )
        copy.start()
        sent.append(copy)

    def arrived(slot, part):
        span = pl.ds(part * half, half)
        pltpu.make_async_remote_copy(
            src_ref=buf.at[slot, span],
            dst_ref=buf.at[slot, span],
            send_sem=ssem.at[0],
            recv_sem=rsem.at[slot * 2 + part],
            device_id=(ctx, partner),
            device_id_type=MESH,
        ).wait_recv()

    def multiply(src, owner, part, mode="add"):
        w_rows = pl.ds(pl.multiple_of(owner * depth, depth), depth)
        tile = min(256, half)

        def step(i, carry):
            span = pl.ds(pl.multiple_of(part * half + i * tile, tile), tile)
            term = dot(src[span, :], wv[w_rows, :])
            if mode == "first":
                acc[span, :] = term
            elif mode == "last":
                o_ref[span, :] = (acc[span, :] + term).astype(o_ref.dtype)
            else:
                acc[span, :] += term
            return carry

        lax.fori_loop(0, half // tile, step, 0)

    send(x_ref, 0, 0, right)
    send(x_ref, 1, 1, left)
    send(x_ref, 3, 0, partner)
    send(x_ref, 3, 1, partner)
    send(x_ref, 0, 1, right)
    send(x_ref, 1, 0, left)
    w_copy.wait()
    multiply(x_ref, me, 0, "first")
    multiply(x_ref, me, 1, "first")
    for part in (0, 1):
        arrived(3, part)
        multiply(buf.at[3], owners[3], part)
    arrived(0, 0)
    send(buf.at[0], 2, 0, right)
    send(buf.at[0], 4, 0, partner)
    arrived(1, 1)
    send(buf.at[1], 2, 1, left)
    send(buf.at[1], 5, 1, partner)
    multiply(buf.at[0], owners[0], 0)
    multiply(buf.at[1], owners[1], 1)
    arrived(4, 0)
    multiply(buf.at[4], owners[4], 0)
    arrived(5, 1)
    multiply(buf.at[5], owners[5], 1)
    arrived(0, 1)
    send(buf.at[0], 4, 1, partner)
    arrived(1, 0)
    send(buf.at[1], 5, 0, partner)
    multiply(buf.at[0], owners[0], 1)
    multiply(buf.at[1], owners[1], 0)
    arrived(4, 1)
    multiply(buf.at[4], owners[4], 1)
    arrived(5, 0)
    multiply(buf.at[5], owners[5], 0)
    arrived(2, 0)
    send(buf.at[2], 6, 0, partner)
    arrived(2, 1)
    send(buf.at[2], 6, 1, partner)
    multiply(buf.at[2], owners[2], 0)
    multiply(buf.at[2], owners[2], 1)
    for part in (0, 1):
        arrived(6, part)
        multiply(buf.at[6], owners[6], part, "last")
    for copy in sent:
        copy.wait_send()


def gather_matmul(x, w, name, collective_id):
    rows, depth = x.shape
    cols = w.shape[1]
    return pl.pallas_call(
        gather_matmul_kernel,
        out_shape=jax.ShapeDtypeStruct((rows, cols), BF16),
        in_specs=[pl.BlockSpec(memory_space=pltpu.VMEM), pl.BlockSpec(memory_space=pl.ANY)],
        out_specs=pl.BlockSpec(memory_space=pltpu.VMEM),
        scratch_shapes=[
            pltpu.VMEM((7, rows, depth), BF16),
            pltpu.VMEM(w.shape, BF16),
            pltpu.VMEM((rows, cols), F32),
            pltpu.SemaphoreType.DMA,
            pltpu.SemaphoreType.DMA((14,)),
            pltpu.SemaphoreType.DMA((14,)),
        ],
        compiler_params=pltpu.CompilerParams(
            collective_id=collective_id, has_side_effects=True, vmem_limit_bytes=48 << 20
        ),
        name=name,
    )(x, w)


def rms_unit(values, eps):
    return values * lax.rsqrt(jnp.mean(values * values, axis=-1, keepdims=True) + eps)


def mix_kernel(
    nz,
    nx,
    p_ref,
    cw_ref,
    gain_ref,
    wo_ref,
    sel_ref,
    col_ref,
    row_ref,
    m_ref,
    wcol_ref,
    halo,
    raw,
    cv,
    kh,
    qh,
    fk,
    fq,
    own,
    win,
    mine,
    zbuf,
    tot,
    xbuf,
    pre,
    wcs,
    hsem,
    zsend,
    zrecv,
    xsend,
    xrecv,
    wsend,
    wrecv,
    wloc,
):
    ctx = lax.axis_index("ctx")
    me = lax.axis_index("head")
    n_ctx = nz * nx
    n_head = 8
    rows = p_ref.shape[0]
    per_head = 2 * FQK + 3 * DV
    out_rows = wo_ref.shape[0]
    out_cols = wo_ref.shape[1] // n_head
    x = lax.div(ctx, nz)
    z = lax.rem(ctx, nz)
    after, before = lax.rem(ctx + 1, n_ctx), lax.rem(ctx + n_ctx - 1, n_ctx)

    def z_peer(d):
        return (x * nz + lax.rem(z + d, nz), me)

    def x_peer(d):
        return (lax.rem(x + d, nx) * nz + z, me)

    barrier = pltpu.get_barrier_semaphore()

    def greet(dev):
        pl.semaphore_signal(barrier, inc=1, device_id=dev, device_id_type=MESH)

    greet((after, me))
    greet((before, me))

    @pl.loop(1, nz)
    def _(d):
        greet(z_peer(d))

    for d in range(1, nx):
        greet(x_peer(d))
    for d in range(1, n_head):
        greet((ctx, lax.rem(me + d, n_head)))
    pl.semaphore_wait(barrier, 2 + (nz - 1) + (nx - 1) + (n_head - 1))

    halo_copy = pltpu.make_async_remote_copy(
        src_ref=p_ref.at[pl.ds(rows - HALO, HALO)],
        dst_ref=halo,
        send_sem=hsem.at[0],
        recv_sem=hsem.at[1],
        device_id=(after, me),
        device_id_type=MESH,
    )
    halo_copy.start()

    def weight_copy(d):
        dev = lax.rem(me + d, n_head)
        return pltpu.make_async_remote_copy(
            src_ref=wo_ref.at[:, pl.ds(pl.multiple_of(dev * out_cols, out_cols), out_cols)],
            dst_ref=wcs.at[pl.ds(pl.multiple_of(me * out_rows, out_rows), out_rows)],
            send_sem=wsend.at[d],
            recv_sem=wrecv.at[d],
            device_id=(ctx, dev),
            device_id_type=MESH,
        )

    own_weight = pltpu.make_async_copy(
        wo_ref.at[:, pl.ds(pl.multiple_of(me * out_cols, out_cols), out_cols)],
        wcs.at[pl.ds(pl.multiple_of(me * out_rows, out_rows), out_rows)],
        wloc,
    )
    own_weight.start()
    for d in range(1, n_head):
        weight_copy(d).start()

    for h in range(2):
        base = h * per_head
        lanes = slice(h * DV, (h + 1) * DV)
        key = p_ref[:, base + FQK : base + 2 * FQK]
        a = dot_nt(sel_ref[0], key)
        b = dot_nt(sel_ref[1], key)
        fk[h] = (col_ref[:, 0:1] * a * (b + col_ref[:, 1:2]) + col_ref[:, 2:3]).astype(BF16)
        at = base + 2 * FQK
        raw[HALO:, lanes] = p_ref[:, at : at + DV].astype(F32)

    halo_copy.wait()
    for h in range(2):
        at = h * per_head + 2 * FQK
        lanes = slice(h * DV, (h + 1) * DV)
        raw[:HALO, lanes] = jnp.where(ctx > 0, halo[:, at : at + DV].astype(F32), 0.0)
    n_ext = rows + WIN
    lead = HALO - WIN
    total = cw_ref[0:1, :] * raw[lead : lead + n_ext, :]
    for j in range(1, CONV):
        total = total + cw_ref[j : j + 1, :] * raw[lead - j : lead - j + n_ext, :]
    cv[...] = total.astype(BF16)

    for h in range(2):
        lanes = slice(h * DV, (h + 1) * DV)
        mine[:, lanes] = dot(fk[h], cv[WIN:, lanes]).astype(BF16)

    def z_copy(d):
        return pltpu.make_async_remote_copy(
            src_ref=mine,
            dst_ref=zbuf.at[d],
            send_sem=zsend.at[d],
            recv_sem=zrecv.at[d],
            device_id=z_peer(d),
            device_id_type=MESH,
        )

    @pl.loop(1, nz)
    def _(d):
        z_copy(d).start()

    for h in range(2):
        base = h * per_head
        lanes = slice(h * DV, (h + 1) * DV)
        at = base + 2 * FQK + DV
        qh[:, lanes] = rms_unit(p_ref[:, at : at + DV].astype(F32), 1e-6).astype(BF16)
        at = at + DV
        kh[WIN:, lanes] = rms_unit(p_ref[:, at : at + DV].astype(F32), 1e-6).astype(BF16)
        kh[:WIN, lanes] = rms_unit(halo[lead:, at : at + DV].astype(F32), 1e-6).astype(BF16)

    wb = 128
    r_id = lax.broadcasted_iota(jnp.int32, (wb, wb + WIN), 0)
    c_id = lax.broadcasted_iota(jnp.int32, (wb, wb + WIN), 1)
    band = (c_id > r_id) & (c_id <= r_id + WIN)

    def window_block(i, carry):
        start = pl.multiple_of(i * wb, wb)
        valid = band & (ctx * rows + start - WIN + c_id >= 0)
        for h in range(2):
            lanes = slice(h * DV, (h + 1) * DV)
            scores = dot_nt(qh[pl.ds(start, wb), lanes], kh[pl.ds(start, wb + WIN), lanes])
            expo = jnp.where(valid, jnp.exp(scores * (1.0 / DV**0.5)), 0.0)
            weights = (expo * (1.0 / jnp.sum(expo, axis=-1, keepdims=True))).astype(BF16)
            win[pl.ds(start, wb), lanes] = dot(weights, cv[pl.ds(start, wb + WIN), lanes])
        return carry

    lax.fori_loop(0, rows // wb, window_block, 0)

    qb = min(256, rows)
    below = lax.broadcasted_iota(jnp.int32, (qb, qb), 1) <= lax.broadcasted_iota(
        jnp.int32, (qb, qb), 0
    )

    def local_linear(h):
        base = h * per_head
        lanes = slice(h * DV, (h + 1) * DV)
        for i in range(rows // qb):
            query = p_ref[i * qb : (i + 1) * qb, base : base + FQK]
            result = None
            for s0, s1 in ((0, i * qb), (i * qb, (i + 1) * qb)):
                if s1 == s0:
                    continue
                u = dot_nt(query, p_ref[s0:s1, base + FQK : base + 2 * FQK]) * (1.0 / FQK**0.5)
                kern = 1.0 + u + 0.5 * u * u
                if s0 == i * qb:
                    kern = jnp.where(below, kern, 0.0)
                term = dot(kern.astype(BF16), cv[WIN + s0 : WIN + s1, lanes])
                result = term if result is None else result + term
            own[i * qb : (i + 1) * qb, lanes] = result

    local_linear(0)

    pre[...] = jnp.zeros_like(pre)
    pre2 = mine[...].astype(F32)

    def z_step(d, total):
        z_copy(d).wait_recv()
        part = zbuf[d].astype(F32)
        pre[...] += jnp.where(d <= z, part, 0.0)
        return total + part

    plane = lax.fori_loop(1, nz, z_step, pre2)
    tot[...] = plane.astype(BF16)

    def x_copy(d):
        return pltpu.make_async_remote_copy(
            src_ref=tot,
            dst_ref=xbuf.at[d],
            send_sem=xsend.at[d],
            recv_sem=xrecv.at[d],
            device_id=x_peer(d),
            device_id_type=MESH,
        )

    for d in range(1, nx):
        x_copy(d).start()

    for h in range(2):
        base = h * per_head
        query = p_ref[:, base : base + FQK]
        a = dot_nt(query, sel_ref[0])
        b = dot_nt(query, sel_ref[1])
        fq[h] = (row_ref[0:1, :] * a * (b + row_ref[1:2, :]) + row_ref[2:3, :]).astype(BF16)
    local_linear(1)

    for d in range(1, nx):
        x_copy(d).wait_recv()
        pre[...] += jnp.where(d <= x, xbuf[d].astype(F32), 0.0)

    for h in range(2):
        lanes = slice(h * DV, (h + 1) * DV)
        lin = own[:, lanes] + dot(fq[h], pre[:, lanes].astype(BF16))
        unit = rms_unit(lin, 1e-5)
        m_ref[:, lanes] = (unit * gain_ref[:, lanes] + win[:, lanes]).astype(BF16)

    own_weight.wait()
    for d in range(1, n_head):
        weight_copy(d).wait()
    wcol_ref[...] = wcs[...]

    @pl.loop(1, nz)
    def _(d):
        z_copy(d).wait_send()

    for d in range(1, nx):
        x_copy(d).wait_send()


def per_device(hidden_in, proj_weight, conv_weight, norm_gain, out_weight):
    rows = hidden_in.shape[0]
    n_ctx = lax.axis_size("ctx")
    nz = NZ
    nx = n_ctx // nz
    width = conv_weight.shape[1]
    n_head = lax.axis_size("head")
    out_rows = out_weight.shape[0]
    out_cols = out_weight.shape[1] // n_head
    sel, coef = feature_tables()
    projected = gather_matmul(hidden_in, proj_weight, "gather_project", 0)
    vmem = pl.BlockSpec(memory_space=pltpu.VMEM)
    dma = pltpu.SemaphoreType.DMA
    mixed, out_cols_weight = pl.pallas_call(
        functools.partial(mix_kernel, nz, nx),
        out_shape=(
            jax.ShapeDtypeStruct((rows, width), BF16),
            jax.ShapeDtypeStruct((out_rows * n_head, out_cols), BF16),
        ),
        in_specs=[vmem] * 7,
        out_specs=(vmem, vmem),
        scratch_shapes=[
            pltpu.VMEM((HALO, projected.shape[1]), BF16),
            pltpu.VMEM((rows + HALO, width), F32),
            pltpu.VMEM((rows + WIN, width), BF16),
            pltpu.VMEM((rows + WIN, width), BF16),
            pltpu.VMEM((rows, width), BF16),
            pltpu.VMEM((2, FEAT, rows), BF16),
            pltpu.VMEM((2, rows, FEAT), BF16),
            pltpu.VMEM((rows, width), F32),
            pltpu.VMEM((rows, width), F32),
            pltpu.VMEM((FEAT, width), BF16),
            pltpu.VMEM((nz, FEAT, width), BF16),
            pltpu.VMEM((FEAT, width), BF16),
            pltpu.VMEM((nx, FEAT, width), BF16),
            pltpu.VMEM((FEAT, width), F32),
            pltpu.VMEM((out_rows * n_head, out_cols), BF16),
            dma((2,)),
            dma((nz,)),
            dma((nz,)),
            dma((nx,)),
            dma((nx,)),
            dma((n_head,)),
            dma((n_head,)),
            dma,
        ],
        compiler_params=pltpu.CompilerParams(
            collective_id=1, has_side_effects=True, vmem_limit_bytes=56 << 20
        ),
        name="mix",
    )(
        projected,
        conv_weight,
        norm_gain.reshape(1, width),
        out_weight,
        jnp.asarray(sel, BF16),
        jnp.asarray(coef.T),
        jnp.asarray(coef),
    )
    return gather_matmul(mixed, out_cols_weight, "gather_out", 2)


def solution(mesh):
    return jax.shard_map(
        per_device,
        mesh=mesh,
        in_specs=(P("ctx", "head"), P(None, "head"), P(None, "head"), P("head"), P("head", None)),
        out_specs=P("ctx", "head"),
        check_vma=False,
    )
```

```python
import functools

import jax
import jax.numpy as jnp
import numpy as np
from jax import lax
from jax.experimental import pallas as pl
from jax.experimental.pallas import tpu as pltpu
from jax.sharding import PartitionSpec as P

DV = 64
FQK = 16
WIN = 64
CONV = 3
NZ = 16
HALO = 80
FEAT = 160
SLICE = 16
OWNER_Z = tuple(s * 8 // 5 for s in range(FEAT // SLICE))
MESH = pl.DeviceIdType.MESH
F32 = jnp.float32
BF16 = jnp.bfloat16
NT = (((1,), (1,)), ((), ()))


def feature_tables():
    first = np.zeros((FEAT, FQK), np.float32)
    second = np.zeros((FEAT, FQK), np.float32)
    coef = np.zeros((3, FEAT), np.float32)
    row = 0
    for i in range(FQK):
        for j in range(i, FQK):
            first[row, i] = 1.0
            second[row, j] = 1.0
            coef[0, row] = (1.0 if i == j else 2.0**0.5) / (2.0 * FQK) ** 0.5
            row += 1
    for i in range(FQK):
        first[row, i] = 1.0
        coef[0, row] = 1.0 / FQK**0.25
        coef[1, row] = 1.0
        row += 1
    coef[2, row] = 1.0
    return np.stack([first, second]), coef


def dot(a, b):
    return jnp.dot(a, b, preferred_element_type=F32)


def dot_nt(a, b):
    return lax.dot_general(a, b, NT, preferred_element_type=F32)


def rms_unit(values, eps):
    return values * lax.rsqrt(jnp.mean(values * values, axis=-1, keepdims=True) + eps)


def ring_gather(x_ref, buf, ctx, me, multiply, ssem, rsem, after_start):
    half = x_ref.shape[0] // 2
    y = lax.div(me, 2)
    core = lax.rem(me, 2)
    other = 1 - core
    y_left, y_right, y_far = lax.rem(y + 3, 4), lax.rem(y + 1, 4), lax.rem(y + 2, 4)
    left, right = y_left * 2 + core, y_right * 2 + core
    partner = y * 2 + other
    owners = [
        left,
        right,
        y_far * 2 + core,
        partner,
        y_left * 2 + other,
        y_right * 2 + other,
        y_far * 2 + other,
    ]
    sent = []

    def send(src, slot, part, dev):
        span = pl.ds(part * half, half)
        copy = pltpu.make_async_remote_copy(
            src_ref=src.at[span],
            dst_ref=buf.at[slot, span],
            send_sem=ssem.at[len(sent)],
            recv_sem=rsem.at[slot * 2 + part],
            device_id=(ctx, dev),
            device_id_type=MESH,
        )
        copy.start()
        sent.append(copy)

    def arrived(slot, part):
        span = pl.ds(part * half, half)
        pltpu.make_async_remote_copy(
            src_ref=buf.at[slot, span],
            dst_ref=buf.at[slot, span],
            send_sem=ssem.at[0],
            recv_sem=rsem.at[slot * 2 + part],
            device_id=(ctx, partner),
            device_id_type=MESH,
        ).wait_recv()

    def use(slot, part, mode="add"):
        multiply(buf.at[slot], owners[slot], part, mode)

    send(x_ref, 0, 0, right)
    send(x_ref, 1, 1, left)
    send(x_ref, 3, 0, partner)
    send(x_ref, 3, 1, partner)
    send(x_ref, 0, 1, right)
    send(x_ref, 1, 0, left)
    after_start()
    for part in (0, 1):
        arrived(3, part)
        use(3, part)
    arrived(0, 0)
    send(buf.at[0], 2, 0, right)
    send(buf.at[0], 4, 0, partner)
    arrived(1, 1)
    send(buf.at[1], 2, 1, left)
    send(buf.at[1], 5, 1, partner)
    use(0, 0)
    use(1, 1)
    arrived(4, 0)
    use(4, 0)
    arrived(5, 1)
    use(5, 1)
    arrived(0, 1)
    send(buf.at[0], 4, 1, partner)
    arrived(1, 0)
    send(buf.at[1], 5, 0, partner)
    use(0, 1)
    use(1, 0)
    arrived(4, 1)
    use(4, 1)
    arrived(5, 0)
    use(5, 0)
    arrived(2, 0)
    send(buf.at[2], 6, 0, partner)
    arrived(2, 1)
    send(buf.at[2], 6, 1, partner)
    use(2, 1)
    use(2, 0)
    for part in (1, 0):
        arrived(6, part)
        use(6, part, "last")
    return sent


def make_multiply(acc, o_ref, half, product):
    tile = min(256, half)

    def multiply(src, owner, part, mode="add"):
        def step(i, carry):
            span = pl.ds(pl.multiple_of(part * half + i * tile, tile), tile)
            term = product(src[span, :], owner)
            if mode == "first":
                acc[span, :] = term
            elif mode == "last":
                o_ref[span, :] = (acc[span, :] + term).astype(o_ref.dtype)
            else:
                acc[span, :] += term
            return carry

        lax.fori_loop(0, half // tile, step, 0)

    return multiply


def layer_kernel(
    nz,
    nx,
    x_ref,
    pw_hbm,
    cw_ref,
    gain_ref,
    wo_ref,
    sel_ref,
    col_ref,
    row_ref,
    o_ref,
    buf_in,
    pwv,
    acc_in,
    p_ref,
    halo,
    raw,
    cv,
    kh,
    qh,
    fk,
    fq,
    own,
    win,
    mine,
    zin,
    zpre,
    zout,
    tot,
    xbuf,
    prior,
    wcs,
    mixed,
    buf_out,
    acc_out,
    pwsem,
    ssem_in,
    rsem_in,
    hsem,
    zsend,
    zrecv,
    xsend,
    xrecv,
    bsend,
    brecv,
    wsend,
    wrecv,
    wloc,
    ssem_out,
    rsem_out,
):
    ctx = lax.axis_index("ctx")
    me = lax.axis_index("head")
    n_ctx = nz * nx
    n_head = 8
    rows, depth = x_ref.shape
    half = rows // 2
    width = cw_ref.shape[1]
    per_head = 2 * FQK + 3 * DV
    out_rows = wo_ref.shape[0]
    out_cols = wo_ref.shape[1] // n_head
    x = lax.div(ctx, nz)
    z = lax.rem(ctx, nz)
    after, before = lax.rem(ctx + 1, n_ctx), lax.rem(ctx + n_ctx - 1, n_ctx)

    pw_copy = pltpu.make_async_copy(pw_hbm, pwv, pwsem)
    pw_copy.start()
    barrier = pltpu.get_barrier_semaphore()

    def greet(dev):
        pl.semaphore_signal(barrier, inc=1, device_id=dev, device_id_type=MESH)

    @pl.loop(1, nz)
    def _(d):
        greet((x * nz + lax.rem(z + d, nz), me))

    greet((after, me))
    greet((before, me))
    for d in range(1, nx):
        greet((lax.rem(x + d, nx) * nz + z, me))
    for d in range(1, n_head):
        greet((ctx, lax.rem(me + d, n_head)))

    def project(part, owner):
        return dot_nt(part, pwv[:, pl.ds(pl.multiple_of(owner * depth, depth), depth)])

    multiply_in = make_multiply(acc_in, p_ref, half, project)
    pw_copy.wait()
    multiply_in(x_ref, me, 0, "first")
    multiply_in(x_ref, me, 1, "first")
    pl.semaphore_wait(barrier, 2 + (nz - 1) + (nx - 1) + (n_head - 1))

    sent = ring_gather(x_ref, buf_in, ctx, me, multiply_in, ssem_in, rsem_in, lambda: None)

    halo_copy = pltpu.make_async_remote_copy(
        src_ref=p_ref.at[pl.ds(rows - HALO, HALO)],
        dst_ref=halo,
        send_sem=hsem.at[0],
        recv_sem=hsem.at[1],
        device_id=(after, me),
        device_id_type=MESH,
    )
    halo_copy.start()

    def weight_copy(d):
        dev = lax.rem(me + d, n_head)
        return pltpu.make_async_remote_copy(
            src_ref=wo_ref.at[:, pl.ds(pl.multiple_of(dev * out_cols, out_cols), out_cols)],
            dst_ref=wcs.at[pl.ds(pl.multiple_of(me * out_rows, out_rows), out_rows)],
            send_sem=wsend.at[d],
            recv_sem=wrecv.at[d],
            device_id=(ctx, dev),
            device_id_type=MESH,
        )

    own_weight = pltpu.make_async_copy(
        wo_ref.at[:, pl.ds(pl.multiple_of(me * out_cols, out_cols), out_cols)],
        wcs.at[pl.ds(pl.multiple_of(me * out_rows, out_rows), out_rows)],
        wloc,
    )
    own_weight.start()
    for d in range(1, n_head):
        weight_copy(d).start()

    for h in range(2):
        base = h * per_head
        lanes = slice(h * DV, (h + 1) * DV)
        key = p_ref[:, base + FQK : base + 2 * FQK]
        a = dot_nt(sel_ref[0], key)
        b = dot_nt(sel_ref[1], key)
        fk[h] = (col_ref[:, 0:1] * a * (b + col_ref[:, 1:2]) + col_ref[:, 2:3]).astype(BF16)
        at = base + 2 * FQK
        raw[HALO:, lanes] = p_ref[:, at : at + DV].astype(F32)

    halo_copy.wait()
    for h in range(2):
        at = h * per_head + 2 * FQK
        lanes = slice(h * DV, (h + 1) * DV)
        raw[:HALO, lanes] = jnp.where(ctx > 0, halo[:, at : at + DV].astype(F32), 0.0)
    n_ext = rows + WIN
    lead = HALO - WIN
    total = cw_ref[0:1, :] * raw[lead : lead + n_ext, :]
    for j in range(1, CONV):
        total = total + cw_ref[j : j + 1, :] * raw[lead - j : lead - j + n_ext, :]
    cv[...] = total.astype(BF16)

    for h in range(2):
        lanes = slice(h * DV, (h + 1) * DV)
        mine[:, lanes] = dot(fk[h], cv[WIN:, lanes]).astype(BF16)

    def to_owner(s):
        return pltpu.make_async_remote_copy(
            src_ref=mine.at[pl.ds(s * SLICE, SLICE)],
            dst_ref=zin.at[z],
            send_sem=zsend.at[s],
            recv_sem=zrecv.at[z],
            device_id=(x * nz + OWNER_Z[s], me),
            device_id_type=MESH,
        )

    for s, z_owner in enumerate(OWNER_Z):

        @pl.when(z != z_owner)
        def _(s=s):
            to_owner(s).start()

        @pl.when(z == z_owner)
        def _(s=s):
            zin[z] = mine[s * SLICE : (s + 1) * SLICE, :]

    for h in range(2):
        base = h * per_head
        lanes = slice(h * DV, (h + 1) * DV)
        at = base + 2 * FQK + DV
        qh[:, lanes] = rms_unit(p_ref[:, at : at + DV].astype(F32), 1e-6).astype(BF16)
        at = at + DV
        kh[WIN:, lanes] = rms_unit(p_ref[:, at : at + DV].astype(F32), 1e-6).astype(BF16)
        kh[:WIN, lanes] = rms_unit(halo[lead:, at : at + DV].astype(F32), 1e-6).astype(BF16)

    wb = 128
    r_id = lax.broadcasted_iota(jnp.int32, (wb, wb + WIN), 0)
    c_id = lax.broadcasted_iota(jnp.int32, (wb, wb + WIN), 1)
    band = (c_id > r_id) & (c_id <= r_id + WIN)

    def window_block(i, carry):
        start = pl.multiple_of(i * wb, wb)
        valid = band & (ctx * rows + start - WIN + c_id >= 0)
        for h in range(2):
            lanes = slice(h * DV, (h + 1) * DV)
            scores = dot_nt(qh[pl.ds(start, wb), lanes], kh[pl.ds(start, wb + WIN), lanes])
            expo = jnp.where(valid, jnp.exp(scores * (1.0 / DV**0.5)), 0.0)
            weights = (expo * (1.0 / jnp.sum(expo, axis=-1, keepdims=True))).astype(BF16)
            win[pl.ds(start, wb), lanes] = dot(weights, cv[pl.ds(start, wb + WIN), lanes])
        return carry

    lax.fori_loop(0, rows // wb, window_block, 0)

    qb = min(256, rows)
    below = lax.broadcasted_iota(jnp.int32, (qb, qb), 1) <= lax.broadcasted_iota(
        jnp.int32, (qb, qb), 0
    )

    def local_linear(h):
        base = h * per_head
        lanes = slice(h * DV, (h + 1) * DV)
        for i in range(rows // qb):
            query = p_ref[i * qb : (i + 1) * qb, base : base + FQK]
            result = None
            for s0, s1 in ((0, i * qb), (i * qb, (i + 1) * qb)):
                if s1 == s0:
                    continue
                u = dot_nt(query, p_ref[s0:s1, base + FQK : base + 2 * FQK]) * (1.0 / FQK**0.5)
                kern = 1.0 + u + 0.5 * u * u
                if s0 == i * qb:
                    kern = jnp.where(below, kern, 0.0)
                term = dot(kern.astype(BF16), cv[WIN + s0 : WIN + s1, lanes])
                result = term if result is None else result + term
            own[i * qb : (i + 1) * qb, lanes] = result

    local_linear(0)

    my_slice = lax.div(z * 5 + 7, 8)
    is_owner = lax.div(my_slice * 8, 5) == z

    def x_copy(d):
        return pltpu.make_async_remote_copy(
            src_ref=tot,
            dst_ref=xbuf.at[d],
            send_sem=xsend.at[d],
            recv_sem=xrecv.at[d],
            device_id=(lax.rem(x + d, nx) * nz + z, me),
            device_id_type=MESH,
        )

    def from_peer(peer):
        return pltpu.make_async_remote_copy(
            src_ref=mine.at[pl.ds(0, SLICE)],
            dst_ref=zin.at[peer],
            send_sem=zsend.at[0],
            recv_sem=zrecv.at[peer],
            device_id=(x * nz + peer, me),
            device_id_type=MESH,
        )

    def back(peer):
        return pltpu.make_async_remote_copy(
            src_ref=zout.at[peer],
            dst_ref=prior.at[pl.ds(pl.multiple_of(my_slice * SLICE, SLICE), SLICE)],
            send_sem=bsend.at[peer],
            recv_sem=brecv.at[my_slice],
            device_id=(x * nz + peer, me),
            device_id_type=MESH,
        )

    def back_from(s):
        return pltpu.make_async_remote_copy(
            src_ref=zout.at[0],
            dst_ref=prior.at[pl.ds(s * SLICE, SLICE)],
            send_sem=bsend.at[0],
            recv_sem=brecv.at[s],
            device_id=(x * nz + OWNER_Z[s], me),
            device_id_type=MESH,
        )

    @pl.when(is_owner)
    def _():
        def scan(peer, run):
            @pl.when(peer != z)
            def _():
                from_peer(peer).wait_recv()

            zpre[peer] = run
            return run + zin[peer].astype(F32)

        plane = lax.fori_loop(0, nz, scan, jnp.zeros((SLICE, width), F32))
        tot[...] = plane.astype(BF16)
        for d in range(1, nx):
            x_copy(d).start()

    for h in range(2):
        base = h * per_head
        query = p_ref[:, base : base + FQK]
        a = dot_nt(query, sel_ref[0])
        b = dot_nt(query, sel_ref[1])
        fq[h] = (row_ref[0:1, :] * a * (b + row_ref[1:2, :]) + row_ref[2:3, :]).astype(BF16)

    @pl.when(is_owner)
    def _():
        planes = jnp.zeros((SLICE, width), F32)
        for d in range(1, nx):
            x_copy(d).wait_recv()
            planes += jnp.where(d <= x, xbuf[d].astype(F32), 0.0)

        def answer(peer, planes):
            value = (zpre[peer] + planes).astype(BF16)
            zout[peer] = value

            @pl.when(peer != z)
            def _():
                back(peer).start()

            @pl.when(peer == z)
            def _():
                prior[pl.ds(pl.multiple_of(my_slice * SLICE, SLICE), SLICE), :] = value

            return planes

        lax.fori_loop(0, nz, answer, planes)

    local_linear(1)

    own_weight.wait()
    for d in range(1, n_head):
        weight_copy(d).wait_recv()
    for s, z_owner in enumerate(OWNER_Z):

        @pl.when(z != z_owner)
        def _(s=s):
            back_from(s).wait_recv()

    for h in range(2):
        lanes = slice(h * DV, (h + 1) * DV)
        lin = own[:, lanes] + dot(fq[h], prior[:, lanes])
        unit = rms_unit(lin, 1e-5)
        mixed[:, lanes] = (unit * gain_ref[:, lanes] + win[:, lanes]).astype(BF16)

    def out_product(part, owner):
        return dot(part, wcs[pl.ds(pl.multiple_of(owner * out_rows, out_rows), out_rows), :])

    multiply_out = make_multiply(acc_out, o_ref, half, out_product)

    def own_out():
        multiply_out(mixed, me, 0, "first")
        multiply_out(mixed, me, 1, "first")

    sent += ring_gather(mixed, buf_out, ctx, me, multiply_out, ssem_out, rsem_out, own_out)

    for copy in sent:
        copy.wait_send()
    for d in range(1, n_head):
        weight_copy(d).wait_send()
    for s, z_owner in enumerate(OWNER_Z):

        @pl.when(z != z_owner)
        def _(s=s):
            to_owner(s).wait_send()

    @pl.when(is_owner)
    def _():
        for d in range(1, nx):
            x_copy(d).wait_send()

        @pl.loop(0, nz)
        def _(peer):
            @pl.when(peer != z)
            def _():
                back(peer).wait_send()


def per_device(hidden_in, proj_weight, conv_weight, norm_gain, out_weight):
    rows, depth = hidden_in.shape
    nz = NZ
    nx = lax.axis_size("ctx") // nz
    width = conv_weight.shape[1]
    cols = proj_weight.shape[1]
    n_head = lax.axis_size("head")
    out_rows = out_weight.shape[0]
    out_cols = out_weight.shape[1] // n_head
    sel, coef = feature_tables()
    vmem = pl.BlockSpec(memory_space=pltpu.VMEM)
    dma = pltpu.SemaphoreType.DMA
    return pl.pallas_call(
        functools.partial(layer_kernel, nz, nx),
        out_shape=jax.ShapeDtypeStruct((rows, out_cols), BF16),
        in_specs=[vmem, pl.BlockSpec(memory_space=pl.ANY)] + [vmem] * 6,
        out_specs=vmem,
        scratch_shapes=[
            pltpu.VMEM((7, rows, depth), BF16),
            pltpu.VMEM((cols, depth * n_head), BF16),
            pltpu.VMEM((rows, cols), F32),
            pltpu.VMEM((rows, cols), BF16),
            pltpu.VMEM((HALO, cols), BF16),
            pltpu.VMEM((rows + HALO, width), F32),
            pltpu.VMEM((rows + WIN, width), BF16),
            pltpu.VMEM((rows + WIN, width), BF16),
            pltpu.VMEM((rows, width), BF16),
            pltpu.VMEM((2, FEAT, rows), BF16),
            pltpu.VMEM((2, rows, FEAT), BF16),
            pltpu.VMEM((rows, width), F32),
            pltpu.VMEM((rows, width), F32),
            pltpu.VMEM((FEAT, width), BF16),
            pltpu.VMEM((nz, SLICE, width), BF16),
            pltpu.VMEM((nz, SLICE, width), F32),
            pltpu.VMEM((nz, SLICE, width), BF16),
            pltpu.VMEM((SLICE, width), BF16),
            pltpu.VMEM((nx, SLICE, width), BF16),
            pltpu.VMEM((FEAT, width), BF16),
            pltpu.VMEM((out_rows * n_head, out_cols), BF16),
            pltpu.VMEM((rows, width), BF16),
            pltpu.VMEM((7, rows, width), BF16),
            pltpu.VMEM((rows, out_cols), F32),
            dma,
            dma((14,)),
            dma((14,)),
            dma((2,)),
            dma((len(OWNER_Z),)),
            dma((nz,)),
            dma((nx,)),
            dma((nx,)),
            dma((nz,)),
            dma((len(OWNER_Z),)),
            dma((n_head,)),
            dma((n_head,)),
            dma,
            dma((14,)),
            dma((14,)),
        ],
        compiler_params=pltpu.CompilerParams(
            collective_id=0, has_side_effects=True, vmem_limit_bytes=56 << 20
        ),
        name="layer",
    )(
        hidden_in,
        proj_weight.T,
        conv_weight,
        norm_gain.reshape(1, width),
        out_weight,
        jnp.asarray(sel, BF16),
        jnp.asarray(coef.T),
        jnp.asarray(coef),
    )


def solution(mesh):
    return jax.shard_map(
        per_device,
        mesh=mesh,
        in_specs=(P("ctx", "head"), P(None, "head"), P(None, "head"), P("head"), P("head", None)),
        out_specs=P("ctx", "head"),
        check_vma=False,
    )
```

```python
import functools

import jax
import jax.numpy as jnp
import numpy as np
from jax import lax
from jax.experimental import pallas as pl
from jax.experimental.pallas import tpu as pltpu
from jax.sharding import PartitionSpec as P

DV = 64
FQK = 16
WIN = 64
CONV = 3
NZ = 16
HALO = 80
FEAT = 160
SLICE = 16
OWNER_Z = tuple(s * 8 // 5 for s in range(FEAT // SLICE))
PARTS = 4
MESH = pl.DeviceIdType.MESH
F32 = jnp.float32
BF16 = jnp.bfloat16
NT = (((1,), (1,)), ((), ()))


def feature_tables():
    first = np.zeros((FEAT, FQK), np.float32)
    second = np.zeros((FEAT, FQK), np.float32)
    coef = np.zeros((3, FEAT), np.float32)
    row = 0
    for i in range(FQK):
        for j in range(i, FQK):
            first[row, i] = 1.0
            second[row, j] = 1.0
            coef[0, row] = (1.0 if i == j else 2.0**0.5) / (2.0 * FQK) ** 0.5
            row += 1
    for i in range(FQK):
        first[row, i] = 1.0
        coef[0, row] = 1.0 / FQK**0.25
        coef[1, row] = 1.0
        row += 1
    coef[2, row] = 1.0
    return np.stack([first, second]), coef


def dot(a, b):
    return jnp.dot(a, b, preferred_element_type=F32)


def dot_nt(a, b):
    return lax.dot_general(a, b, NT, preferred_element_type=F32)


def rms_unit(values, eps):
    return values * lax.rsqrt(jnp.mean(values * values, axis=-1, keepdims=True) + eps)


def ring_gather(x_ref, buf, ctx, me, multiply, ssem, rsem, ready, after_start):
    size = x_ref.shape[0] // PARTS
    y = lax.div(me, 2)
    core = lax.rem(me, 2)
    other = 1 - core
    y_left, y_right, y_far = lax.rem(y + 3, 4), lax.rem(y + 1, 4), lax.rem(y + 2, 4)
    left, right = y_left * 2 + core, y_right * 2 + core
    partner = y * 2 + other
    owners = [
        left,
        right,
        y_far * 2 + core,
        partner,
        y_left * 2 + other,
        y_right * 2 + other,
        y_far * 2 + other,
    ]
    sent = []

    def send(src, slot, part, dev):
        span = pl.ds(part * size, size)
        copy = pltpu.make_async_remote_copy(
            src_ref=src.at[span],
            dst_ref=buf.at[slot, span],
            send_sem=ssem.at[len(sent)],
            recv_sem=rsem.at[slot * PARTS + part],
            device_id=(ctx, dev),
            device_id_type=MESH,
        )
        copy.start()
        sent.append(copy)

    def arrived(slot, part):
        span = pl.ds(part * size, size)
        pltpu.make_async_remote_copy(
            src_ref=buf.at[slot, span],
            dst_ref=buf.at[slot, span],
            send_sem=ssem.at[0],
            recv_sem=rsem.at[slot * PARTS + part],
            device_id=(ctx, partner),
            device_id_type=MESH,
        ).wait_recv()

    def use(slot, part, mode="add"):
        multiply(buf.at[slot], owners[slot], part, mode)

    lower = list(range(PARTS // 2))
    upper = list(range(PARTS // 2, PARTS))
    for part in lower:
        ready(part)
        send(x_ref, 0, part, right)
    for part in upper:
        ready(part)
        send(x_ref, 1, part, left)
    for part in upper:
        send(x_ref, 0, part, right)
    for part in lower:
        send(x_ref, 1, part, left)
    for part in lower + upper:
        send(x_ref, 3, part, partner)
    after_start()
    for part in lower + upper:
        arrived(3, part)
        use(3, part)
    for lo, up in zip(lower, upper):
        arrived(0, lo)
        send(buf.at[0], 2, lo, right)
        send(buf.at[0], 4, lo, partner)
        arrived(1, up)
        send(buf.at[1], 2, up, left)
        send(buf.at[1], 5, up, partner)
        use(0, lo)
        use(1, up)
    for lo, up in zip(lower, upper):
        arrived(4, lo)
        use(4, lo)
        arrived(5, up)
        use(5, up)
    for lo, up in zip(lower, upper):
        arrived(0, up)
        send(buf.at[0], 4, up, partner)
        arrived(1, lo)
        send(buf.at[1], 5, lo, partner)
        use(0, up)
        use(1, lo)
    for lo, up in zip(lower, upper):
        arrived(4, up)
        use(4, up)
        arrived(5, lo)
        use(5, lo)
    for lo, up in zip(lower, upper):
        arrived(2, lo)
        send(buf.at[2], 6, lo, partner)
        arrived(2, up)
        send(buf.at[2], 6, up, partner)
        use(2, up)
        use(2, lo)
    for lo, up in zip(lower, upper):
        for part in (up, lo):
            arrived(6, part)
            use(6, part, "last")
    return sent


def make_multiply(acc, o_ref, size, product):
    tile = min(256, size)

    def multiply(src, owner, part, mode="add"):
        def step(i, carry):
            span = pl.ds(pl.multiple_of(part * size + i * tile, tile), tile)
            term = product(src[span, :], owner)
            if mode == "first":
                acc[span, :] = term
            elif mode == "last":
                o_ref[span, :] = (acc[span, :] + term).astype(o_ref.dtype)
            else:
                acc[span, :] += term
            return carry

        lax.fori_loop(0, size // tile, step, 0)

    return multiply


def layer_kernel(
    nz,
    nx,
    x_hbm,
    pw_hbm,
    cw_hbm,
    gain_hbm,
    wo_hbm,
    sel_hbm,
    col_hbm,
    row_hbm,
    o_ref,
    x_ref,
    cw_ref,
    gain_ref,
    wo_ref,
    sel_ref,
    col_ref,
    row_ref,
    buf_in,
    pwv,
    acc_in,
    p_ref,
    halo,
    raw,
    cv,
    kh,
    qh,
    fk,
    fq,
    own,
    win,
    mine,
    zin,
    zpre,
    zout,
    tot,
    xbuf,
    prior,
    wcs,
    mixed,
    buf_out,
    acc_out,
    pwsem,
    insem,
    ssem_in,
    rsem_in,
    hsem,
    zsend,
    zrecv,
    xsend,
    xrecv,
    bsend,
    brecv,
    wsend,
    wrecv,
    wloc,
    ssem_out,
    rsem_out,
):
    ctx = lax.axis_index("ctx")
    me = lax.axis_index("head")
    n_ctx = nz * nx
    n_head = 8
    rows, depth = x_ref.shape
    size = rows // PARTS
    width = cw_ref.shape[1]
    per_head = 2 * FQK + 3 * DV
    out_rows = wo_ref.shape[0]
    out_cols = wo_ref.shape[1] // n_head
    x = lax.div(ctx, nz)
    z = lax.rem(ctx, nz)
    after, before = lax.rem(ctx + 1, n_ctx), lax.rem(ctx + n_ctx - 1, n_ctx)

    barrier = pltpu.get_barrier_semaphore()

    def greet(dev):
        pl.semaphore_signal(barrier, inc=1, device_id=dev, device_id_type=MESH)

    @pl.loop(1, nz)
    def _(d):
        greet((x * nz + lax.rem(z + d, nz), me))

    greet((after, me))
    greet((before, me))
    for d in range(1, nx):
        greet((lax.rem(x + d, nx) * nz + z, me))
    for d in range(1, n_head):
        greet((ctx, lax.rem(me + d, n_head)))

    x_copy_in = pltpu.make_async_copy(x_hbm, x_ref, insem.at[0])
    x_copy_in.start()
    pw_copy = pltpu.make_async_copy(pw_hbm, pwv, pwsem)
    pw_copy.start()
    late = [(cw_hbm, cw_ref), (gain_hbm, gain_ref), (wo_hbm, wo_ref)]
    late += [(sel_hbm, sel_ref), (col_hbm, col_ref), (row_hbm, row_ref)]
    late = [pltpu.make_async_copy(a, b, insem.at[k + 1]) for k, (a, b) in enumerate(late)]
    for copy in late:
        copy.start()
    x_copy_in.wait()

    def project(part, owner):
        return dot_nt(part, pwv[:, pl.ds(pl.multiple_of(owner * depth, depth), depth)])

    multiply_in = make_multiply(acc_in, p_ref, size, project)
    pw_copy.wait()
    for part in range(PARTS):
        multiply_in(x_ref, me, part, "first")
    pl.semaphore_wait(barrier, 2 + (nz - 1) + (nx - 1) + (n_head - 1))

    sent = ring_gather(x_ref, buf_in, ctx, me, multiply_in, ssem_in, rsem_in, lambda part: None, lambda: None)

    halo_copy = pltpu.make_async_remote_copy(
        src_ref=p_ref.at[pl.ds(rows - HALO, HALO)],
        dst_ref=halo,
        send_sem=hsem.at[0],
        recv_sem=hsem.at[1],
        device_id=(after, me),
        device_id_type=MESH,
    )
    halo_copy.start()
    for copy in late:
        copy.wait()

    def weight_copy(d):
        dev = lax.rem(me + d, n_head)
        return pltpu.make_async_remote_copy(
            src_ref=wo_ref.at[:, pl.ds(pl.multiple_of(dev * out_cols, out_cols), out_cols)],
            dst_ref=wcs.at[pl.ds(pl.multiple_of(me * out_rows, out_rows), out_rows)],
            send_sem=wsend.at[d],
            recv_sem=wrecv.at[d],
            device_id=(ctx, dev),
            device_id_type=MESH,
        )

    own_weight = pltpu.make_async_copy(
        wo_ref.at[:, pl.ds(pl.multiple_of(me * out_cols, out_cols), out_cols)],
        wcs.at[pl.ds(pl.multiple_of(me * out_rows, out_rows), out_rows)],
        wloc,
    )
    own_weight.start()
    for d in range(1, n_head):
        weight_copy(d).start()

    for h in range(2):
        base = h * per_head
        lanes = slice(h * DV, (h + 1) * DV)
        key = p_ref[:, base + FQK : base + 2 * FQK]
        a = dot_nt(sel_ref[0], key)
        b = dot_nt(sel_ref[1], key)
        fk[h] = (col_ref[:, 0:1] * a * (b + col_ref[:, 1:2]) + col_ref[:, 2:3]).astype(BF16)
        at = base + 2 * FQK
        raw[HALO:, lanes] = p_ref[:, at : at + DV].astype(F32)

    lead = HALO - WIN
    head_rows = 128

    def convolve(first, count):
        total = cw_ref[0:1, :] * raw[lead + first : lead + first + count, :]
        for j in range(1, CONV):
            at = lead + first - j
            total = total + cw_ref[j : j + 1, :] * raw[at : at + count, :]
        cv[first : first + count, :] = total.astype(BF16)

    def state(first, count, h):
        lanes = slice(h * DV, (h + 1) * DV)
        return dot(
            fk[h, :, first : first + count], cv[WIN + first : WIN + first + count, lanes]
        )

    convolve(WIN + head_rows, rows - head_rows)
    main = [state(head_rows, rows - head_rows, h) for h in range(2)]
    halo_copy.wait()
    for h in range(2):
        at = h * per_head + 2 * FQK
        lanes = slice(h * DV, (h + 1) * DV)
        raw[:HALO, lanes] = jnp.where(ctx > 0, halo[:, at : at + DV].astype(F32), 0.0)
    convolve(0, WIN + head_rows)
    for h in range(2):
        lanes = slice(h * DV, (h + 1) * DV)
        mine[:, lanes] = (main[h] + state(0, head_rows, h)).astype(BF16)

    def to_owner(s):
        return pltpu.make_async_remote_copy(
            src_ref=mine.at[pl.ds(s * SLICE, SLICE)],
            dst_ref=zin.at[z],
            send_sem=zsend.at[s],
            recv_sem=zrecv.at[z],
            device_id=(x * nz + OWNER_Z[s], me),
            device_id_type=MESH,
        )

    for s, z_owner in enumerate(OWNER_Z):

        @pl.when(z != z_owner)
        def _(s=s):
            to_owner(s).start()

        @pl.when(z == z_owner)
        def _(s=s):
            zin[z] = mine[s * SLICE : (s + 1) * SLICE, :]

    for h in range(2):
        base = h * per_head
        lanes = slice(h * DV, (h + 1) * DV)
        at = base + 2 * FQK + DV
        qh[:, lanes] = rms_unit(p_ref[:, at : at + DV].astype(F32), 1e-6).astype(BF16)
        at = at + DV
        kh[WIN:, lanes] = rms_unit(p_ref[:, at : at + DV].astype(F32), 1e-6).astype(BF16)
        kh[:WIN, lanes] = rms_unit(halo[lead:, at : at + DV].astype(F32), 1e-6).astype(BF16)

    wb = 128
    r_id = lax.broadcasted_iota(jnp.int32, (wb, wb + WIN), 0)
    c_id = lax.broadcasted_iota(jnp.int32, (wb, wb + WIN), 1)
    band = (c_id > r_id) & (c_id <= r_id + WIN)

    def window_block(i, carry):
        start = pl.multiple_of(i * wb, wb)
        valid = band & (ctx * rows + start - WIN + c_id >= 0)
        for h in range(2):
            lanes = slice(h * DV, (h + 1) * DV)
            scores = dot_nt(qh[pl.ds(start, wb), lanes], kh[pl.ds(start, wb + WIN), lanes])
            expo = jnp.where(valid, jnp.exp(scores * (1.0 / DV**0.5)), 0.0)
            weights = (expo * (1.0 / jnp.sum(expo, axis=-1, keepdims=True))).astype(BF16)
            win[pl.ds(start, wb), lanes] = dot(weights, cv[pl.ds(start, wb + WIN), lanes])
        return carry

    lax.fori_loop(0, rows // wb, window_block, 0)

    qb = min(256, rows)
    below = lax.broadcasted_iota(jnp.int32, (qb, qb), 1) <= lax.broadcasted_iota(
        jnp.int32, (qb, qb), 0
    )

    def local_linear(h):
        base = h * per_head
        lanes = slice(h * DV, (h + 1) * DV)
        for i in range(rows // qb):
            query = p_ref[i * qb : (i + 1) * qb, base : base + FQK]
            result = None
            for s0, s1 in ((0, i * qb), (i * qb, (i + 1) * qb)):
                if s1 == s0:
                    continue
                u = dot_nt(query, p_ref[s0:s1, base + FQK : base + 2 * FQK]) * (1.0 / FQK**0.5)
                kern = 1.0 + u + 0.5 * u * u
                if s0 == i * qb:
                    kern = jnp.where(below, kern, 0.0)
                term = dot(kern.astype(BF16), cv[WIN + s0 : WIN + s1, lanes])
                result = term if result is None else result + term
            own[i * qb : (i + 1) * qb, lanes] = result

    local_linear(0)

    my_slice = lax.div(z * 5 + 7, 8)
    is_owner = lax.div(my_slice * 8, 5) == z

    def x_copy(d):
        return pltpu.make_async_remote_copy(
            src_ref=tot,
            dst_ref=xbuf.at[d],
            send_sem=xsend.at[d],
            recv_sem=xrecv.at[d],
            device_id=(lax.rem(x + d, nx) * nz + z, me),
            device_id_type=MESH,
        )

    def from_peer(peer):
        return pltpu.make_async_remote_copy(
            src_ref=mine.at[pl.ds(0, SLICE)],
            dst_ref=zin.at[peer],
            send_sem=zsend.at[0],
            recv_sem=zrecv.at[peer],
            device_id=(x * nz + peer, me),
            device_id_type=MESH,
        )

    def back(peer):
        return pltpu.make_async_remote_copy(
            src_ref=zout.at[peer],
            dst_ref=prior.at[pl.ds(pl.multiple_of(my_slice * SLICE, SLICE), SLICE)],
            send_sem=bsend.at[peer],
            recv_sem=brecv.at[my_slice],
            device_id=(x * nz + peer, me),
            device_id_type=MESH,
        )

    def back_from(s):
        return pltpu.make_async_remote_copy(
            src_ref=zout.at[0],
            dst_ref=prior.at[pl.ds(s * SLICE, SLICE)],
            send_sem=bsend.at[0],
            recv_sem=brecv.at[s],
            device_id=(x * nz + OWNER_Z[s], me),
            device_id_type=MESH,
        )

    @pl.when(is_owner)
    def _():
        def scan(peer, run):
            @pl.when(peer != z)
            def _():
                from_peer(peer).wait_recv()

            zpre[peer] = run
            return run + zin[peer].astype(F32)

        plane = lax.fori_loop(0, nz, scan, jnp.zeros((SLICE, width), F32))
        tot[...] = plane.astype(BF16)
        for d in range(1, nx):
            x_copy(d).start()

    for h in range(2):
        base = h * per_head
        query = p_ref[:, base : base + FQK]
        a = dot_nt(query, sel_ref[0])
        b = dot_nt(query, sel_ref[1])
        fq[h] = (row_ref[0:1, :] * a * (b + row_ref[1:2, :]) + row_ref[2:3, :]).astype(BF16)

    @pl.when(is_owner)
    def _():
        planes = jnp.zeros((SLICE, width), F32)
        for d in range(1, nx):
            x_copy(d).wait_recv()
            planes += jnp.where(d <= x, xbuf[d].astype(F32), 0.0)

        def answer(peer, planes):
            value = (zpre[peer] + planes).astype(BF16)
            zout[peer] = value

            @pl.when(peer != z)
            def _():
                back(peer).start()

            @pl.when(peer == z)
            def _():
                prior[pl.ds(pl.multiple_of(my_slice * SLICE, SLICE), SLICE), :] = value

            return planes

        lax.fori_loop(0, nz, answer, planes)

    local_linear(1)

    own_weight.wait()
    for d in range(1, n_head):
        weight_copy(d).wait_recv()
    for s, z_owner in enumerate(OWNER_Z):

        @pl.when(z != z_owner)
        def _(s=s):
            back_from(s).wait_recv()

    def mix_part(part):
        span = slice(part * size, (part + 1) * size)
        for h in range(2):
            lanes = slice(h * DV, (h + 1) * DV)
            lin = own[span, lanes] + dot(fq[h, span, :], prior[:, lanes])
            unit = rms_unit(lin, 1e-5)
            mixed[span, lanes] = (unit * gain_ref[:, lanes] + win[span, lanes]).astype(BF16)

    def out_product(part, owner):
        return dot(part, wcs[pl.ds(pl.multiple_of(owner * out_rows, out_rows), out_rows), :])

    multiply_out = make_multiply(acc_out, o_ref, size, out_product)

    def own_out():
        for part in range(PARTS):
            multiply_out(mixed, me, part, "first")

    sent += ring_gather(mixed, buf_out, ctx, me, multiply_out, ssem_out, rsem_out, mix_part, own_out)

    for copy in sent:
        copy.wait_send()
    for d in range(1, n_head):
        weight_copy(d).wait_send()
    for s, z_owner in enumerate(OWNER_Z):

        @pl.when(z != z_owner)
        def _(s=s):
            to_owner(s).wait_send()

    @pl.when(is_owner)
    def _():
        for d in range(1, nx):
            x_copy(d).wait_send()

        @pl.loop(0, nz)
        def _(peer):
            @pl.when(peer != z)
            def _():
                back(peer).wait_send()


def per_device(hidden_in, proj_weight, conv_weight, norm_gain, out_weight):
    rows, depth = hidden_in.shape
    nz = NZ
    nx = lax.axis_size("ctx") // nz
    width = conv_weight.shape[1]
    cols = proj_weight.shape[1]
    n_head = lax.axis_size("head")
    out_rows = out_weight.shape[0]
    out_cols = out_weight.shape[1] // n_head
    sel, coef = feature_tables()
    vmem = pl.BlockSpec(memory_space=pltpu.VMEM)
    dma = pltpu.SemaphoreType.DMA
    return pl.pallas_call(
        functools.partial(layer_kernel, nz, nx),
        out_shape=jax.ShapeDtypeStruct((rows, out_cols), BF16),
        in_specs=[pl.BlockSpec(memory_space=pltpu.HBM)] * 8,
        out_specs=vmem,
        scratch_shapes=[
            pltpu.VMEM((rows, depth), BF16),
            pltpu.VMEM(conv_weight.shape, F32),
            pltpu.VMEM((1, width), F32),
            pltpu.VMEM(out_weight.shape, BF16),
            pltpu.VMEM(sel.shape, BF16),
            pltpu.VMEM(coef.T.shape, F32),
            pltpu.VMEM(coef.shape, F32),
            pltpu.VMEM((7, rows, depth), BF16),
            pltpu.VMEM((cols, depth * n_head), BF16),
            pltpu.VMEM((rows, cols), F32),
            pltpu.VMEM((rows, cols), BF16),
            pltpu.VMEM((HALO, cols), BF16),
            pltpu.VMEM((rows + HALO, width), F32),
            pltpu.VMEM((rows + WIN, width), BF16),
            pltpu.VMEM((rows + WIN, width), BF16),
            pltpu.VMEM((rows, width), BF16),
            pltpu.VMEM((2, FEAT, rows), BF16),
            pltpu.VMEM((2, rows, FEAT), BF16),
            pltpu.VMEM((rows, width), F32),
            pltpu.VMEM((rows, width), F32),
            pltpu.VMEM((FEAT, width), BF16),
            pltpu.VMEM((nz, SLICE, width), BF16),
            pltpu.VMEM((nz, SLICE, width), F32),
            pltpu.VMEM((nz, SLICE, width), BF16),
            pltpu.VMEM((SLICE, width), BF16),
            pltpu.VMEM((nx, SLICE, width), BF16),
            pltpu.VMEM((FEAT, width), BF16),
            pltpu.VMEM((out_rows * n_head, out_cols), BF16),
            pltpu.VMEM((rows, width), BF16),
            pltpu.VMEM((7, rows, width), BF16),
            pltpu.VMEM((rows, out_cols), F32),
            dma,
            dma((7,)),
            dma((7 * PARTS,)),
            dma((7 * PARTS,)),
            dma((2,)),
            dma((len(OWNER_Z),)),
            dma((nz,)),
            dma((nx,)),
            dma((nx,)),
            dma((nz,)),
            dma((len(OWNER_Z),)),
            dma((n_head,)),
            dma((n_head,)),
            dma,
            dma((7 * PARTS,)),
            dma((7 * PARTS,)),
        ],
        compiler_params=pltpu.CompilerParams(
            collective_id=0, has_side_effects=True, vmem_limit_bytes=58000000
        ),
        name="layer",
    )(
        hidden_in,
        proj_weight.T,
        conv_weight,
        norm_gain.reshape(1, width),
        out_weight,
        jnp.asarray(sel, BF16),
        jnp.asarray(coef.T),
        jnp.asarray(coef),
    )


def solution(mesh):
    return jax.shard_map(
        per_device,
        mesh=mesh,
        in_specs=(P("ctx", "head"), P(None, "head"), P(None, "head"), P("head"), P("head", None)),
        out_specs=P("ctx", "head"),
        check_vma=False,
    )
```

```python
import functools

import jax
import jax.numpy as jnp
import numpy as np
from jax import lax
from jax.experimental import pallas as pl
from jax.experimental.pallas import tpu as pltpu
from jax.sharding import PartitionSpec as P

DV = 64
FQK = 16
WIN = 64
CONV = 3
NZ = 16
HALO = 80
FEAT = 160
SLICE = 16
OWNER_Z = tuple(s * 8 // 5 for s in range(FEAT // SLICE))
PARTS = 4
MESH = pl.DeviceIdType.MESH
F32 = jnp.float32
BF16 = jnp.bfloat16
NT = (((1,), (1,)), ((), ()))


def feature_tables():
    first = np.zeros((FEAT, FQK), np.float32)
    second = np.zeros((FEAT, FQK), np.float32)
    coef = np.zeros((3, FEAT), np.float32)
    row = 0
    for i in range(FQK):
        for j in range(i, FQK):
            first[row, i] = 1.0
            second[row, j] = 1.0
            coef[0, row] = (1.0 if i == j else 2.0**0.5) / (2.0 * FQK) ** 0.5
            row += 1
    for i in range(FQK):
        first[row, i] = 1.0
        coef[0, row] = 1.0 / FQK**0.25
        coef[1, row] = 1.0
        row += 1
    coef[2, row] = 1.0
    return np.stack([first, second]), coef


def dot(a, b):
    return jnp.dot(a, b, preferred_element_type=F32)


def dot_nt(a, b):
    return lax.dot_general(a, b, NT, preferred_element_type=F32)


def rms_unit(values, eps):
    return values * lax.rsqrt(jnp.mean(values * values, axis=-1, keepdims=True) + eps)


def ring_gather(x_ref, buf, ctx, me, multiply, ssem, rsem, ready, after_start, tick):
    size = x_ref.shape[0] // PARTS
    y = lax.div(me, 2)
    core = lax.rem(me, 2)
    other = 1 - core
    y_left, y_right, y_far = lax.rem(y + 3, 4), lax.rem(y + 1, 4), lax.rem(y + 2, 4)
    left, right = y_left * 2 + core, y_right * 2 + core
    partner = y * 2 + other
    owners = [
        left,
        right,
        y_far * 2 + core,
        partner,
        y_left * 2 + other,
        y_right * 2 + other,
        y_far * 2 + other,
    ]
    sent = []

    def send(src, slot, part, dev):
        span = pl.ds(part * size, size)
        copy = pltpu.make_async_remote_copy(
            src_ref=src.at[span],
            dst_ref=buf.at[slot, span],
            send_sem=ssem.at[len(sent)],
            recv_sem=rsem.at[slot * PARTS + part],
            device_id=(ctx, dev),
            device_id_type=MESH,
        )
        copy.start()
        sent.append(copy)

    def arrived(slot, part):
        span = pl.ds(part * size, size)
        pltpu.make_async_remote_copy(
            src_ref=buf.at[slot, span],
            dst_ref=buf.at[slot, span],
            send_sem=ssem.at[0],
            recv_sem=rsem.at[slot * PARTS + part],
            device_id=(ctx, partner),
            device_id_type=MESH,
        ).wait_recv()

    def use(slot, part, mode="add"):
        multiply(buf.at[slot], owners[slot], part, mode)

    lower = list(range(PARTS // 2))
    upper = list(range(PARTS // 2, PARTS))
    for part in lower:
        ready(part)
        send(x_ref, 0, part, right)
    for part in upper:
        ready(part)
        send(x_ref, 1, part, left)
    for part in upper:
        send(x_ref, 0, part, right)
    for part in lower:
        send(x_ref, 1, part, left)
    for part in lower + upper:
        send(x_ref, 3, part, partner)
    after_start()
    for part in lower + upper:
        arrived(3, part)
        use(3, part)
    for lo, up in zip(lower, upper):
        arrived(0, lo)
        send(buf.at[0], 2, lo, right)
        send(buf.at[0], 4, lo, partner)
        arrived(1, up)
        send(buf.at[1], 2, up, left)
        send(buf.at[1], 5, up, partner)
        use(0, lo)
        use(1, up)
        tick()
    for lo, up in zip(lower, upper):
        arrived(4, lo)
        use(4, lo)
        arrived(5, up)
        use(5, up)
        tick()
    for lo, up in zip(lower, upper):
        arrived(0, up)
        send(buf.at[0], 4, up, partner)
        arrived(1, lo)
        send(buf.at[1], 5, lo, partner)
        use(0, up)
        use(1, lo)
        tick()
    for lo, up in zip(lower, upper):
        arrived(4, up)
        use(4, up)
        arrived(5, lo)
        use(5, lo)
        tick()
    for lo, up in zip(lower, upper):
        arrived(2, lo)
        send(buf.at[2], 6, lo, partner)
        arrived(2, up)
        send(buf.at[2], 6, up, partner)
        use(2, up)
        use(2, lo)
    for lo, up in zip(lower, upper):
        for part in (up, lo):
            arrived(6, part)
            use(6, part, "last")
    return sent


def make_multiply(acc, o_ref, size, product):
    tile = min(256, size)

    def multiply(src, owner, part, mode="add"):
        def step(i, carry):
            span = pl.ds(pl.multiple_of(part * size + i * tile, tile), tile)
            term = product(src[span, :], owner)
            if mode == "first":
                acc[span, :] = term
            elif mode == "last":
                o_ref[span, :] = (acc[span, :] + term).astype(o_ref.dtype)
            else:
                acc[span, :] += term
            return carry

        lax.fori_loop(0, size // tile, step, 0)

    return multiply


def layer_kernel(
    nz,
    nx,
    x_hbm,
    pw_hbm,
    cw_hbm,
    gain_hbm,
    wo_hbm,
    sel_hbm,
    col_hbm,
    row_hbm,
    o_ref,
    x_ref,
    cw_ref,
    gain_ref,
    wo_ref,
    sel_ref,
    col_ref,
    row_ref,
    buf_in,
    pwv,
    acc_in,
    p_ref,
    halo,
    raw,
    cv,
    kh,
    qh,
    fk,
    fq,
    own,
    win,
    mine,
    zin,
    zpre,
    zout,
    tot,
    xbuf,
    prior,
    wcs,
    mixed,
    buf_out,
    acc_out,
    pwsem,
    insem,
    ssem_in,
    rsem_in,
    hsem,
    zsend,
    zrecv,
    xsend,
    xrecv,
    bsend,
    brecv,
    wsend,
    wrecv,
    wloc,
    ssem_out,
    rsem_out,
    tokens,
):
    ctx = lax.axis_index("ctx")
    me = lax.axis_index("head")
    n_ctx = nz * nx
    n_head = 8
    rows, depth = x_ref.shape
    size = rows // PARTS
    width = cw_ref.shape[1]
    per_head = 2 * FQK + 3 * DV
    out_rows = wo_ref.shape[0]
    out_cols = wo_ref.shape[1] // n_head
    x = lax.div(ctx, nz)
    z = lax.rem(ctx, nz)
    after, before = lax.rem(ctx + 1, n_ctx), lax.rem(ctx + n_ctx - 1, n_ctx)

    barrier = pltpu.get_barrier_semaphore()

    def greet(dev):
        pl.semaphore_signal(barrier, inc=1, device_id=dev, device_id_type=MESH)

    z_sides = ((x * nz + lax.rem(z + 1, nz), me), (x * nz + lax.rem(z + nz - 1, nz), me))
    for dev in z_sides:
        greet(dev)
    greet((after, me))
    greet((before, me))
    for d in range(1, nx):
        greet((lax.rem(x + d, nx) * nz + z, me))
    for d in range(1, n_head):
        greet((ctx, lax.rem(me + d, n_head)))

    x_copy_in = pltpu.make_async_copy(x_hbm, x_ref, insem.at[0])
    x_copy_in.start()
    pw_copy = pltpu.make_async_copy(pw_hbm, pwv, pwsem)
    pw_copy.start()
    late = [(cw_hbm, cw_ref), (gain_hbm, gain_ref), (wo_hbm, wo_ref)]
    late += [(sel_hbm, sel_ref), (col_hbm, col_ref), (row_hbm, row_ref)]
    late = [pltpu.make_async_copy(a, b, insem.at[k + 1]) for k, (a, b) in enumerate(late)]
    for copy in late:
        copy.start()
    x_copy_in.wait()

    def project(part, owner):
        return dot_nt(part, pwv[:, pl.ds(pl.multiple_of(owner * depth, depth), depth)])

    multiply_in = make_multiply(acc_in, p_ref, size, project)
    pw_copy.wait()
    for part in range(PARTS):
        multiply_in(x_ref, me, part, "first")
    pl.semaphore_wait(barrier, 2 + 2 + (nx - 1) + (n_head - 1))

    rounds = nz // 2 - 1
    passed = []

    def tell():
        for dev in z_sides:
            pl.semaphore_signal(
                tokens.at[len(passed)], inc=1, device_id=dev, device_id_type=MESH
            )

    def tick():
        if len(passed) < rounds:
            pl.semaphore_wait(tokens.at[len(passed)], 2)
            passed.append(1)
            if len(passed) < rounds:
                tell()

    tell()

    sent = ring_gather(x_ref, buf_in, ctx, me, multiply_in, ssem_in, rsem_in, lambda part: None, lambda: None, tick)

    halo_copy = pltpu.make_async_remote_copy(
        src_ref=p_ref.at[pl.ds(rows - HALO, HALO)],
        dst_ref=halo,
        send_sem=hsem.at[0],
        recv_sem=hsem.at[1],
        device_id=(after, me),
        device_id_type=MESH,
    )
    halo_copy.start()
    for copy in late:
        copy.wait()

    def weight_copy(d):
        dev = lax.rem(me + d, n_head)
        return pltpu.make_async_remote_copy(
            src_ref=wo_ref.at[:, pl.ds(pl.multiple_of(dev * out_cols, out_cols), out_cols)],
            dst_ref=wcs.at[pl.ds(pl.multiple_of(me * out_rows, out_rows), out_rows)],
            send_sem=wsend.at[d],
            recv_sem=wrecv.at[d],
            device_id=(ctx, dev),
            device_id_type=MESH,
        )

    own_weight = pltpu.make_async_copy(
        wo_ref.at[:, pl.ds(pl.multiple_of(me * out_cols, out_cols), out_cols)],
        wcs.at[pl.ds(pl.multiple_of(me * out_rows, out_rows), out_rows)],
        wloc,
    )
    own_weight.start()
    for d in range(1, n_head):
        weight_copy(d).start()

    for h in range(2):
        base = h * per_head
        lanes = slice(h * DV, (h + 1) * DV)
        key = p_ref[:, base + FQK : base + 2 * FQK]
        a = dot_nt(sel_ref[0], key)
        b = dot_nt(sel_ref[1], key)
        fk[h] = (col_ref[:, 0:1] * a * (b + col_ref[:, 1:2]) + col_ref[:, 2:3]).astype(BF16)
        at = base + 2 * FQK
        raw[HALO:, lanes] = p_ref[:, at : at + DV].astype(F32)

    lead = HALO - WIN
    head_rows = 128

    def convolve(first, count):
        total = cw_ref[0:1, :] * raw[lead + first : lead + first + count, :]
        for j in range(1, CONV):
            at = lead + first - j
            total = total + cw_ref[j : j + 1, :] * raw[at : at + count, :]
        cv[first : first + count, :] = total.astype(BF16)

    def state(first, count, h):
        lanes = slice(h * DV, (h + 1) * DV)
        return dot(
            fk[h, :, first : first + count], cv[WIN + first : WIN + first + count, lanes]
        )

    convolve(WIN + head_rows, rows - head_rows)
    main = [state(head_rows, rows - head_rows, h) for h in range(2)]
    halo_copy.wait()
    for h in range(2):
        at = h * per_head + 2 * FQK
        lanes = slice(h * DV, (h + 1) * DV)
        raw[:HALO, lanes] = jnp.where(ctx > 0, halo[:, at : at + DV].astype(F32), 0.0)
    convolve(0, WIN + head_rows)
    for h in range(2):
        lanes = slice(h * DV, (h + 1) * DV)
        mine[:, lanes] = (main[h] + state(0, head_rows, h)).astype(BF16)

    def to_owner(s):
        return pltpu.make_async_remote_copy(
            src_ref=mine.at[pl.ds(s * SLICE, SLICE)],
            dst_ref=zin.at[z],
            send_sem=zsend.at[s],
            recv_sem=zrecv.at[z],
            device_id=(x * nz + OWNER_Z[s], me),
            device_id_type=MESH,
        )

    for s, z_owner in enumerate(OWNER_Z):

        @pl.when(z != z_owner)
        def _(s=s):
            to_owner(s).start()

        @pl.when(z == z_owner)
        def _(s=s):
            zin[z] = mine[s * SLICE : (s + 1) * SLICE, :]

    for h in range(2):
        base = h * per_head
        lanes = slice(h * DV, (h + 1) * DV)
        at = base + 2 * FQK + DV
        qh[:, lanes] = rms_unit(p_ref[:, at : at + DV].astype(F32), 1e-6).astype(BF16)
        at = at + DV
        kh[WIN:, lanes] = rms_unit(p_ref[:, at : at + DV].astype(F32), 1e-6).astype(BF16)
        kh[:WIN, lanes] = rms_unit(halo[lead:, at : at + DV].astype(F32), 1e-6).astype(BF16)

    wb = 128
    r_id = lax.broadcasted_iota(jnp.int32, (wb, wb + WIN), 0)
    c_id = lax.broadcasted_iota(jnp.int32, (wb, wb + WIN), 1)
    band = (c_id > r_id) & (c_id <= r_id + WIN)

    def window_block(i, carry):
        start = pl.multiple_of(i * wb, wb)
        valid = band & (ctx * rows + start - WIN + c_id >= 0)
        for h in range(2):
            lanes = slice(h * DV, (h + 1) * DV)
            scores = dot_nt(qh[pl.ds(start, wb), lanes], kh[pl.ds(start, wb + WIN), lanes])
            expo = jnp.where(valid, jnp.exp(scores * (1.0 / DV**0.5)), 0.0)
            weights = (expo * (1.0 / jnp.sum(expo, axis=-1, keepdims=True))).astype(BF16)
            win[pl.ds(start, wb), lanes] = dot(weights, cv[pl.ds(start, wb + WIN), lanes])
        return carry

    lax.fori_loop(0, rows // wb, window_block, 0)

    qb = min(256, rows)
    below = lax.broadcasted_iota(jnp.int32, (qb, qb), 1) <= lax.broadcasted_iota(
        jnp.int32, (qb, qb), 0
    )

    def local_linear(h):
        base = h * per_head
        lanes = slice(h * DV, (h + 1) * DV)
        for i in range(rows // qb):
            query = p_ref[i * qb : (i + 1) * qb, base : base + FQK]
            result = None
            for s0, s1 in ((0, i * qb), (i * qb, (i + 1) * qb)):
                if s1 == s0:
                    continue
                u = dot_nt(query, p_ref[s0:s1, base + FQK : base + 2 * FQK]) * (1.0 / FQK**0.5)
                kern = 1.0 + u + 0.5 * u * u
                if s0 == i * qb:
                    kern = jnp.where(below, kern, 0.0)
                term = dot(kern.astype(BF16), cv[WIN + s0 : WIN + s1, lanes])
                result = term if result is None else result + term
            own[i * qb : (i + 1) * qb, lanes] = result

    local_linear(0)

    my_slice = lax.div(z * 5 + 7, 8)
    is_owner = lax.div(my_slice * 8, 5) == z

    def x_copy(d):
        return pltpu.make_async_remote_copy(
            src_ref=tot,
            dst_ref=xbuf.at[d],
            send_sem=xsend.at[d],
            recv_sem=xrecv.at[d],
            device_id=(lax.rem(x + d, nx) * nz + z, me),
            device_id_type=MESH,
        )

    def from_peer(peer):
        return pltpu.make_async_remote_copy(
            src_ref=mine.at[pl.ds(0, SLICE)],
            dst_ref=zin.at[peer],
            send_sem=zsend.at[0],
            recv_sem=zrecv.at[peer],
            device_id=(x * nz + peer, me),
            device_id_type=MESH,
        )

    def back(peer):
        return pltpu.make_async_remote_copy(
            src_ref=zout.at[peer],
            dst_ref=prior.at[pl.ds(pl.multiple_of(my_slice * SLICE, SLICE), SLICE)],
            send_sem=bsend.at[peer],
            recv_sem=brecv.at[my_slice],
            device_id=(x * nz + peer, me),
            device_id_type=MESH,
        )

    def back_from(s):
        return pltpu.make_async_remote_copy(
            src_ref=zout.at[0],
            dst_ref=prior.at[pl.ds(s * SLICE, SLICE)],
            send_sem=bsend.at[0],
            recv_sem=brecv.at[s],
            device_id=(x * nz + OWNER_Z[s], me),
            device_id_type=MESH,
        )

    @pl.when(is_owner)
    def _():
        def scan(peer, run):
            @pl.when(peer != z)
            def _():
                from_peer(peer).wait_recv()

            zpre[peer] = run
            return run + zin[peer].astype(F32)

        plane = lax.fori_loop(0, nz, scan, jnp.zeros((SLICE, width), F32))
        tot[...] = plane.astype(BF16)
        for d in range(1, nx):
            x_copy(d).start()

    for h in range(2):
        base = h * per_head
        query = p_ref[:, base : base + FQK]
        a = dot_nt(query, sel_ref[0])
        b = dot_nt(query, sel_ref[1])
        fq[h] = (row_ref[0:1, :] * a * (b + row_ref[1:2, :]) + row_ref[2:3, :]).astype(BF16)

    @pl.when(is_owner)
    def _():
        planes = jnp.zeros((SLICE, width), F32)
        for d in range(1, nx):
            x_copy(d).wait_recv()
            planes += jnp.where(d <= x, xbuf[d].astype(F32), 0.0)

        def answer(peer, planes):
            value = (zpre[peer] + planes).astype(BF16)
            zout[peer] = value

            @pl.when(peer != z)
            def _():
                back(peer).start()

            @pl.when(peer == z)
            def _():
                prior[pl.ds(pl.multiple_of(my_slice * SLICE, SLICE), SLICE), :] = value

            return planes

        lax.fori_loop(0, nz, answer, planes)

    local_linear(1)

    own_weight.wait()
    for d in range(1, n_head):
        weight_copy(d).wait_recv()
    for s, z_owner in enumerate(OWNER_Z):

        @pl.when(z != z_owner)
        def _(s=s):
            back_from(s).wait_recv()

    def mix_part(part):
        span = slice(part * size, (part + 1) * size)
        for h in range(2):
            lanes = slice(h * DV, (h + 1) * DV)
            lin = own[span, lanes] + dot(fq[h, span, :], prior[:, lanes])
            unit = rms_unit(lin, 1e-5)
            mixed[span, lanes] = (unit * gain_ref[:, lanes] + win[span, lanes]).astype(BF16)

    def out_product(part, owner):
        return dot(part, wcs[pl.ds(pl.multiple_of(owner * out_rows, out_rows), out_rows), :])

    multiply_out = make_multiply(acc_out, o_ref, size, out_product)

    def own_out():
        for part in range(PARTS):
            multiply_out(mixed, me, part, "first")

    sent += ring_gather(mixed, buf_out, ctx, me, multiply_out, ssem_out, rsem_out, mix_part, own_out, lambda: None)

    for copy in sent:
        copy.wait_send()
    for d in range(1, n_head):
        weight_copy(d).wait_send()
    for s, z_owner in enumerate(OWNER_Z):

        @pl.when(z != z_owner)
        def _(s=s):
            to_owner(s).wait_send()

    @pl.when(is_owner)
    def _():
        for d in range(1, nx):
            x_copy(d).wait_send()

        @pl.loop(0, nz)
        def _(peer):
            @pl.when(peer != z)
            def _():
                back(peer).wait_send()


def per_device(hidden_in, proj_weight, conv_weight, norm_gain, out_weight):
    rows, depth = hidden_in.shape
    nz = NZ
    nx = lax.axis_size("ctx") // nz
    width = conv_weight.shape[1]
    cols = proj_weight.shape[1]
    n_head = lax.axis_size("head")
    out_rows = out_weight.shape[0]
    out_cols = out_weight.shape[1] // n_head
    sel, coef = feature_tables()
    vmem = pl.BlockSpec(memory_space=pltpu.VMEM)
    dma = pltpu.SemaphoreType.DMA
    return pl.pallas_call(
        functools.partial(layer_kernel, nz, nx),
        out_shape=jax.ShapeDtypeStruct((rows, out_cols), BF16),
        in_specs=[pl.BlockSpec(memory_space=pltpu.HBM)] * 8,
        out_specs=vmem,
        scratch_shapes=[
            pltpu.VMEM((rows, depth), BF16),
            pltpu.VMEM(conv_weight.shape, F32),
            pltpu.VMEM((1, width), F32),
            pltpu.VMEM(out_weight.shape, BF16),
            pltpu.VMEM(sel.shape, BF16),
            pltpu.VMEM(coef.T.shape, F32),
            pltpu.VMEM(coef.shape, F32),
            pltpu.VMEM((7, rows, depth), BF16),
            pltpu.VMEM((cols, depth * n_head), BF16),
            pltpu.VMEM((rows, cols), F32),
            pltpu.VMEM((rows, cols), BF16),
            pltpu.VMEM((HALO, cols), BF16),
            pltpu.VMEM((rows + HALO, width), F32),
            pltpu.VMEM((rows + WIN, width), BF16),
            pltpu.VMEM((rows + WIN, width), BF16),
            pltpu.VMEM((rows, width), BF16),
            pltpu.VMEM((2, FEAT, rows), BF16),
            pltpu.VMEM((2, rows, FEAT), BF16),
            pltpu.VMEM((rows, width), F32),
            pltpu.VMEM((rows, width), F32),
            pltpu.VMEM((FEAT, width), BF16),
            pltpu.VMEM((nz, SLICE, width), BF16),
            pltpu.VMEM((nz, SLICE, width), F32),
            pltpu.VMEM((nz, SLICE, width), BF16),
            pltpu.VMEM((SLICE, width), BF16),
            pltpu.VMEM((nx, SLICE, width), BF16),
            pltpu.VMEM((FEAT, width), BF16),
            pltpu.VMEM((out_rows * n_head, out_cols), BF16),
            pltpu.VMEM((rows, width), BF16),
            pltpu.VMEM((7, rows, width), BF16),
            pltpu.VMEM((rows, out_cols), F32),
            dma,
            dma((7,)),
            dma((7 * PARTS,)),
            dma((7 * PARTS,)),
            dma((2,)),
            dma((len(OWNER_Z),)),
            dma((nz,)),
            dma((nx,)),
            dma((nx,)),
            dma((nz,)),
            dma((len(OWNER_Z),)),
            dma((n_head,)),
            dma((n_head,)),
            dma,
            dma((7 * PARTS,)),
            dma((7 * PARTS,)),
            pltpu.SemaphoreType.REGULAR((nz // 2 - 1,)),
        ],
        compiler_params=pltpu.CompilerParams(
            collective_id=0, has_side_effects=True, vmem_limit_bytes=48 << 20
        ),
        name="layer",
    )(
        *(
            pltpu.with_memory_space_constraint(value, pltpu.HBM)
            for value in (
                hidden_in,
                proj_weight.T,
                conv_weight,
                norm_gain.reshape(1, width),
                out_weight,
                jnp.asarray(sel, BF16),
                jnp.asarray(coef.T),
                jnp.asarray(coef),
            )
        )
    )


def solution(mesh):
    return jax.shard_map(
        per_device,
        mesh=mesh,
        in_specs=(P("ctx", "head"), P(None, "head"), P(None, "head"), P("head"), P("head", None)),
        out_specs=P("ctx", "head"),
        check_vma=False,
    )
```

```python
import functools

import jax
import jax.numpy as jnp
import numpy as np
from jax import lax
from jax.experimental import pallas as pl
from jax.experimental.pallas import tpu as pltpu
from jax.sharding import PartitionSpec as P

DV = 64
FQK = 16
WIN = 64
CONV = 3
NZ = 16
HALO = 80
FEAT = 160
SLICE = 16
OWNER_Z = tuple(s * 8 // 5 for s in range(FEAT // SLICE))
PARTS = 4
MESH = pl.DeviceIdType.MESH
F32 = jnp.float32
BF16 = jnp.bfloat16
NT = (((1,), (1,)), ((), ()))


def feature_tables():
    first = np.zeros((FEAT, FQK), np.float32)
    second = np.zeros((FEAT, FQK), np.float32)
    coef = np.zeros((3, FEAT), np.float32)
    row = 0
    for i in range(FQK):
        for j in range(i, FQK):
            first[row, i] = 1.0
            second[row, j] = 1.0
            coef[0, row] = (1.0 if i == j else 2.0**0.5) / (2.0 * FQK) ** 0.5
            row += 1
    for i in range(FQK):
        first[row, i] = 1.0
        coef[0, row] = 1.0 / FQK**0.25
        coef[1, row] = 1.0
        row += 1
    coef[2, row] = 1.0
    return np.stack([first, second]), coef


def dot(a, b):
    return jnp.dot(a, b, preferred_element_type=F32)


def dot_nt(a, b):
    return lax.dot_general(a, b, NT, preferred_element_type=F32)


def rms_unit(values, eps):
    return values * lax.rsqrt(jnp.mean(values * values, axis=-1, keepdims=True) + eps)


def ring_gather(x_ref, buf, ctx, me, multiply, ssem, rsem, ready, after_start, tick):
    size = x_ref.shape[0] // PARTS
    y = lax.div(me, 2)
    core = lax.rem(me, 2)
    other = 1 - core
    y_left, y_right, y_far = lax.rem(y + 3, 4), lax.rem(y + 1, 4), lax.rem(y + 2, 4)
    left, right = y_left * 2 + core, y_right * 2 + core
    partner = y * 2 + other
    owners = [
        left,
        right,
        y_far * 2 + core,
        partner,
        y_left * 2 + other,
        y_right * 2 + other,
        y_far * 2 + other,
    ]
    sent = []

    def send(src, slot, part, dev):
        span = pl.ds(part * size, size)
        copy = pltpu.make_async_remote_copy(
            src_ref=src.at[span],
            dst_ref=buf.at[slot, span],
            send_sem=ssem.at[len(sent)],
            recv_sem=rsem.at[slot * PARTS + part],
            device_id=(ctx, dev),
            device_id_type=MESH,
        )
        copy.start()
        sent.append(copy)

    def arrived(slot, part):
        span = pl.ds(part * size, size)
        pltpu.make_async_remote_copy(
            src_ref=buf.at[slot, span],
            dst_ref=buf.at[slot, span],
            send_sem=ssem.at[0],
            recv_sem=rsem.at[slot * PARTS + part],
            device_id=(ctx, partner),
            device_id_type=MESH,
        ).wait_recv()

    def use(slot, part, mode="add"):
        multiply(buf.at[slot], owners[slot], part, mode)

    lower = list(range(PARTS // 2))
    upper = list(range(PARTS // 2, PARTS))
    for part in lower:
        ready(part)
        send(x_ref, 0, part, right)
    for part in upper:
        ready(part)
        send(x_ref, 1, part, left)
    for part in upper:
        send(x_ref, 0, part, right)
    for part in lower:
        send(x_ref, 1, part, left)
    for part in lower + upper:
        send(x_ref, 3, part, partner)
    after_start()
    for part in lower + upper:
        arrived(3, part)
        use(3, part)
    for lo, up in zip(lower, upper):
        arrived(0, lo)
        send(buf.at[0], 2, lo, right)
        send(buf.at[0], 4, lo, partner)
        arrived(1, up)
        send(buf.at[1], 2, up, left)
        send(buf.at[1], 5, up, partner)
        use(0, lo)
        use(1, up)
        tick()
    for lo, up in zip(lower, upper):
        arrived(4, lo)
        use(4, lo)
        arrived(5, up)
        use(5, up)
        tick()
    for lo, up in zip(lower, upper):
        arrived(0, up)
        send(buf.at[0], 4, up, partner)
        arrived(1, lo)
        send(buf.at[1], 5, lo, partner)
        use(0, up)
        use(1, lo)
        tick()
    for lo, up in zip(lower, upper):
        arrived(4, up)
        use(4, up)
        arrived(5, lo)
        use(5, lo)
        tick()
    for lo, up in zip(lower, upper):
        arrived(2, lo)
        send(buf.at[2], 6, lo, partner)
        arrived(2, up)
        send(buf.at[2], 6, up, partner)
        use(2, up)
        use(2, lo)
    for lo, up in zip(lower, upper):
        for part in (up, lo):
            arrived(6, part)
            use(6, part, "last")
    return sent


def make_multiply(acc, o_ref, size, product):
    tile = min(256, size)

    def multiply(src, owner, part, mode="add"):
        def step(i, carry):
            span = pl.ds(pl.multiple_of(part * size + i * tile, tile), tile)
            term = product(src[span, :], owner)
            if mode == "first":
                acc[span, :] = term
            elif mode == "last":
                o_ref[span, :] = (acc[span, :] + term).astype(o_ref.dtype)
            else:
                acc[span, :] += term
            return carry

        lax.fori_loop(0, size // tile, step, 0)

    return multiply


def layer_kernel(
    nz,
    nx,
    x_hbm,
    pw_hbm,
    cw_hbm,
    gain_hbm,
    wo_hbm,
    sel_hbm,
    col_hbm,
    row_hbm,
    o_ref,
    x_ref,
    cw_ref,
    gain_ref,
    wo_ref,
    sel_ref,
    col_ref,
    row_ref,
    buf_in,
    pwv,
    acc_in,
    p_ref,
    halo,
    raw,
    cv,
    kh,
    qh,
    fk,
    fq,
    own,
    win,
    mine,
    zin,
    zpre,
    zout,
    tot,
    xbuf,
    prior,
    wcs,
    mixed,
    buf_out,
    acc_out,
    pwsem,
    insem,
    ssem_in,
    rsem_in,
    hsem,
    zsend,
    zrecv,
    xsend,
    xrecv,
    bsend,
    brecv,
    wsend,
    wrecv,
    wloc,
    ssem_out,
    rsem_out,
    tokens,
):
    ctx = lax.axis_index("ctx")
    me = lax.axis_index("head")
    n_ctx = nz * nx
    n_head = 8
    rows, depth = x_ref.shape
    size = rows // PARTS
    width = cw_ref.shape[1]
    per_head = 2 * FQK + 3 * DV
    out_rows = wo_ref.shape[0]
    out_cols = wo_ref.shape[1] // n_head
    x = lax.div(ctx, nz)
    z = lax.rem(ctx, nz)
    after, before = lax.rem(ctx + 1, n_ctx), lax.rem(ctx + n_ctx - 1, n_ctx)

    barrier = pltpu.get_barrier_semaphore()

    def greet(dev):
        pl.semaphore_signal(barrier, inc=1, device_id=dev, device_id_type=MESH)

    z_sides = ((x * nz + lax.rem(z + 1, nz), me), (x * nz + lax.rem(z + nz - 1, nz), me))
    for dev in z_sides:
        greet(dev)
    greet((after, me))
    greet((before, me))
    for d in range(1, nx):
        greet((lax.rem(x + d, nx) * nz + z, me))
    for d in range(1, n_head):
        greet((ctx, lax.rem(me + d, n_head)))

    x_copy_in = pltpu.make_async_copy(x_hbm, x_ref, insem.at[0])
    x_copy_in.start()
    pw_copy = pltpu.make_async_copy(pw_hbm, pwv, pwsem)
    pw_copy.start()
    late = [(cw_hbm, cw_ref), (gain_hbm, gain_ref), (wo_hbm, wo_ref)]
    late += [(sel_hbm, sel_ref), (col_hbm, col_ref), (row_hbm, row_ref)]
    late = [pltpu.make_async_copy(a, b, insem.at[k + 1]) for k, (a, b) in enumerate(late)]
    for copy in late:
        copy.start()
    x_copy_in.wait()

    def project(part, owner):
        return dot_nt(part, pwv[:, pl.ds(pl.multiple_of(owner * depth, depth), depth)])

    multiply_in = make_multiply(acc_in, p_ref, size, project)
    pw_copy.wait()
    for part in range(PARTS):
        multiply_in(x_ref, me, part, "first")
    pl.semaphore_wait(barrier, 2 + 2 + (nx - 1) + (n_head - 1))

    rounds = nz // 2 - 1
    passed = []

    def tell():
        for dev in z_sides:
            pl.semaphore_signal(
                tokens.at[len(passed)], inc=1, device_id=dev, device_id_type=MESH
            )

    def tick():
        if len(passed) < rounds:
            pl.semaphore_wait(tokens.at[len(passed)], 2)
            passed.append(1)
            if len(passed) < rounds:
                tell()

    tell()

    sent = ring_gather(x_ref, buf_in, ctx, me, multiply_in, ssem_in, rsem_in, lambda part: None, lambda: None, tick)

    halo_copy = pltpu.make_async_remote_copy(
        src_ref=p_ref.at[pl.ds(rows - HALO, HALO)],
        dst_ref=halo,
        send_sem=hsem.at[0],
        recv_sem=hsem.at[1],
        device_id=(after, me),
        device_id_type=MESH,
    )
    halo_copy.start()
    for copy in late:
        copy.wait()

    def weight_copy(d):
        dev = lax.rem(me + d, n_head)
        return pltpu.make_async_remote_copy(
            src_ref=wo_ref.at[:, pl.ds(pl.multiple_of(dev * out_cols, out_cols), out_cols)],
            dst_ref=wcs.at[pl.ds(pl.multiple_of(me * out_rows, out_rows), out_rows)],
            send_sem=wsend.at[d],
            recv_sem=wrecv.at[d],
            device_id=(ctx, dev),
            device_id_type=MESH,
        )

    own_weight = pltpu.make_async_copy(
        wo_ref.at[:, pl.ds(pl.multiple_of(me * out_cols, out_cols), out_cols)],
        wcs.at[pl.ds(pl.multiple_of(me * out_rows, out_rows), out_rows)],
        wloc,
    )
    own_weight.start()
    for d in range(1, n_head):
        weight_copy(d).start()

    for h in range(2):
        base = h * per_head
        lanes = slice(h * DV, (h + 1) * DV)
        key = p_ref[:, base + FQK : base + 2 * FQK]
        a = dot_nt(sel_ref[0], key)
        b = dot_nt(sel_ref[1], key)
        fk[h] = (col_ref[:, 0:1] * a * (b + col_ref[:, 1:2]) + col_ref[:, 2:3]).astype(BF16)
        at = base + 2 * FQK
        raw[HALO:, lanes] = p_ref[:, at : at + DV].astype(F32)

    lead = HALO - WIN
    head_rows = 128

    def convolve(first, count):
        total = cw_ref[0:1, :] * raw[lead + first : lead + first + count, :]
        for j in range(1, CONV):
            at = lead + first - j
            total = total + cw_ref[j : j + 1, :] * raw[at : at + count, :]
        cv[first : first + count, :] = total.astype(BF16)

    def state(first, count, h):
        lanes = slice(h * DV, (h + 1) * DV)
        return dot(
            fk[h, :, first : first + count], cv[WIN + first : WIN + first + count, lanes]
        )

    convolve(WIN + head_rows, rows - head_rows)
    main = [state(head_rows, rows - head_rows, h) for h in range(2)]
    halo_copy.wait()
    for h in range(2):
        at = h * per_head + 2 * FQK
        lanes = slice(h * DV, (h + 1) * DV)
        raw[:HALO, lanes] = jnp.where(ctx > 0, halo[:, at : at + DV].astype(F32), 0.0)
    convolve(0, WIN + head_rows)
    for h in range(2):
        lanes = slice(h * DV, (h + 1) * DV)
        mine[:, lanes] = (main[h] + state(0, head_rows, h)).astype(BF16)

    def to_owner(s):
        return pltpu.make_async_remote_copy(
            src_ref=mine.at[pl.ds(s * SLICE, SLICE)],
            dst_ref=zin.at[z],
            send_sem=zsend.at[s],
            recv_sem=zrecv.at[z],
            device_id=(x * nz + OWNER_Z[s], me),
            device_id_type=MESH,
        )

    for s, z_owner in enumerate(OWNER_Z):

        @pl.when(z != z_owner)
        def _(s=s):
            to_owner(s).start()

        @pl.when(z == z_owner)
        def _(s=s):
            zin[z] = mine[s * SLICE : (s + 1) * SLICE, :]

    for h in range(2):
        base = h * per_head
        lanes = slice(h * DV, (h + 1) * DV)
        at = base + 2 * FQK + DV
        qh[:, lanes] = rms_unit(p_ref[:, at : at + DV].astype(F32), 1e-6).astype(BF16)
        at = at + DV
        kh[WIN:, lanes] = rms_unit(p_ref[:, at : at + DV].astype(F32), 1e-6).astype(BF16)
        kh[:WIN, lanes] = rms_unit(halo[lead:, at : at + DV].astype(F32), 1e-6).astype(BF16)

    wb = 128
    r_id = lax.broadcasted_iota(jnp.int32, (wb, wb + WIN), 0)
    c_id = lax.broadcasted_iota(jnp.int32, (wb, wb + WIN), 1)
    band = (c_id > r_id) & (c_id <= r_id + WIN)

    def window_block(i, carry):
        start = pl.multiple_of(i * wb, wb)
        valid = band & (ctx * rows + start - WIN + c_id >= 0)
        for h in range(2):
            lanes = slice(h * DV, (h + 1) * DV)
            scores = dot_nt(qh[pl.ds(start, wb), lanes], kh[pl.ds(start, wb + WIN), lanes])
            expo = jnp.where(valid, jnp.exp(scores * (1.0 / DV**0.5)), 0.0)
            weights = (expo * (1.0 / jnp.sum(expo, axis=-1, keepdims=True))).astype(BF16)
            win[pl.ds(start, wb), lanes] = dot(weights, cv[pl.ds(start, wb + WIN), lanes])
        return carry

    lax.fori_loop(0, rows // wb, window_block, 0)

    qb = min(256, rows)
    below = lax.broadcasted_iota(jnp.int32, (qb, qb), 1) <= lax.broadcasted_iota(
        jnp.int32, (qb, qb), 0
    )

    def local_linear(h):
        base = h * per_head
        lanes = slice(h * DV, (h + 1) * DV)
        for i in range(rows // qb):
            query = p_ref[i * qb : (i + 1) * qb, base : base + FQK]
            result = None
            for s0, s1 in ((0, i * qb), (i * qb, (i + 1) * qb)):
                if s1 == s0:
                    continue
                u = dot_nt(query, p_ref[s0:s1, base + FQK : base + 2 * FQK]) * (1.0 / FQK**0.5)
                kern = 1.0 + u + 0.5 * u * u
                if s0 == i * qb:
                    kern = jnp.where(below, kern, 0.0)
                term = dot(kern.astype(BF16), cv[WIN + s0 : WIN + s1, lanes])
                result = term if result is None else result + term
            own[i * qb : (i + 1) * qb, lanes] = result

    my_slice = lax.div(z * 5 + 7, 8)
    is_owner = lax.div(my_slice * 8, 5) == z

    def x_copy(d):
        return pltpu.make_async_remote_copy(
            src_ref=tot,
            dst_ref=xbuf.at[d],
            send_sem=xsend.at[d],
            recv_sem=xrecv.at[d],
            device_id=(lax.rem(x + d, nx) * nz + z, me),
            device_id_type=MESH,
        )

    def from_peer(peer):
        return pltpu.make_async_remote_copy(
            src_ref=mine.at[pl.ds(0, SLICE)],
            dst_ref=zin.at[peer],
            send_sem=zsend.at[0],
            recv_sem=zrecv.at[peer],
            device_id=(x * nz + peer, me),
            device_id_type=MESH,
        )

    def back(peer):
        return pltpu.make_async_remote_copy(
            src_ref=zout.at[peer],
            dst_ref=prior.at[pl.ds(pl.multiple_of(my_slice * SLICE, SLICE), SLICE)],
            send_sem=bsend.at[peer],
            recv_sem=brecv.at[my_slice],
            device_id=(x * nz + peer, me),
            device_id_type=MESH,
        )

    def back_from(s):
        return pltpu.make_async_remote_copy(
            src_ref=zout.at[0],
            dst_ref=prior.at[pl.ds(s * SLICE, SLICE)],
            send_sem=bsend.at[0],
            recv_sem=brecv.at[s],
            device_id=(x * nz + OWNER_Z[s], me),
            device_id_type=MESH,
        )

    @pl.when(is_owner)
    def _():
        def scan(peer, run):
            @pl.when(peer != z)
            def _():
                from_peer(peer).wait_recv()

            zpre[peer] = run
            return run + zin[peer].astype(F32)

        plane = lax.fori_loop(0, nz, scan, jnp.zeros((SLICE, width), F32))
        tot[...] = plane.astype(BF16)
        for d in range(1, nx):
            x_copy(d).start()

    @pl.when(is_owner)
    def _():
        planes = jnp.zeros((SLICE, width), F32)
        for d in range(1, nx):
            x_copy(d).wait_recv()
            planes += jnp.where(d <= x, xbuf[d].astype(F32), 0.0)

        def answer(peer, planes):
            value = (zpre[peer] + planes).astype(BF16)
            zout[peer] = value

            @pl.when(peer != z)
            def _():
                back(peer).start()

            @pl.when(peer == z)
            def _():
                prior[pl.ds(pl.multiple_of(my_slice * SLICE, SLICE), SLICE), :] = value

            return planes

        lax.fori_loop(0, nz, answer, planes)

    for h in range(2):
        base = h * per_head
        query = p_ref[:, base : base + FQK]
        a = dot_nt(query, sel_ref[0])
        b = dot_nt(query, sel_ref[1])
        fq[h] = (row_ref[0:1, :] * a * (b + row_ref[1:2, :]) + row_ref[2:3, :]).astype(BF16)

    local_linear(0)
    local_linear(1)

    own_weight.wait()
    for d in range(1, n_head):
        weight_copy(d).wait_recv()
    for s, z_owner in enumerate(OWNER_Z):

        @pl.when(z != z_owner)
        def _(s=s):
            back_from(s).wait_recv()

    def mix_part(part):
        span = slice(part * size, (part + 1) * size)
        for h in range(2):
            lanes = slice(h * DV, (h + 1) * DV)
            lin = own[span, lanes] + dot(fq[h, span, :], prior[:, lanes])
            unit = rms_unit(lin, 1e-5)
            mixed[span, lanes] = (unit * gain_ref[:, lanes] + win[span, lanes]).astype(BF16)

    def out_product(part, owner):
        return dot(part, wcs[pl.ds(pl.multiple_of(owner * out_rows, out_rows), out_rows), :])

    multiply_out = make_multiply(acc_out, o_ref, size, out_product)

    def own_out():
        for part in range(PARTS):
            multiply_out(mixed, me, part, "first")

    sent += ring_gather(mixed, buf_out, ctx, me, multiply_out, ssem_out, rsem_out, mix_part, own_out, lambda: None)

    for copy in sent:
        copy.wait_send()
    for d in range(1, n_head):
        weight_copy(d).wait_send()
    for s, z_owner in enumerate(OWNER_Z):

        @pl.when(z != z_owner)
        def _(s=s):
            to_owner(s).wait_send()

    @pl.when(is_owner)
    def _():
        for d in range(1, nx):
            x_copy(d).wait_send()

        @pl.loop(0, nz)
        def _(peer):
            @pl.when(peer != z)
            def _():
                back(peer).wait_send()


def per_device(hidden_in, proj_weight, conv_weight, norm_gain, out_weight):
    rows, depth = hidden_in.shape
    nz = NZ
    nx = lax.axis_size("ctx") // nz
    width = conv_weight.shape[1]
    cols = proj_weight.shape[1]
    n_head = lax.axis_size("head")
    out_rows = out_weight.shape[0]
    out_cols = out_weight.shape[1] // n_head
    sel, coef = feature_tables()
    vmem = pl.BlockSpec(memory_space=pltpu.VMEM)
    dma = pltpu.SemaphoreType.DMA
    return pl.pallas_call(
        functools.partial(layer_kernel, nz, nx),
        out_shape=jax.ShapeDtypeStruct((rows, out_cols), BF16),
        in_specs=[pl.BlockSpec(memory_space=pltpu.HBM)] * 8,
        out_specs=vmem,
        scratch_shapes=[
            pltpu.VMEM((rows, depth), BF16),
            pltpu.VMEM(conv_weight.shape, F32),
            pltpu.VMEM((1, width), F32),
            pltpu.VMEM(out_weight.shape, BF16),
            pltpu.VMEM(sel.shape, BF16),
            pltpu.VMEM(coef.T.shape, F32),
            pltpu.VMEM(coef.shape, F32),
            pltpu.VMEM((7, rows, depth), BF16),
            pltpu.VMEM((cols, depth * n_head), BF16),
            pltpu.VMEM((rows, cols), F32),
            pltpu.VMEM((rows, cols), BF16),
            pltpu.VMEM((HALO, cols), BF16),
            pltpu.VMEM((rows + HALO, width), F32),
            pltpu.VMEM((rows + WIN, width), BF16),
            pltpu.VMEM((rows + WIN, width), BF16),
            pltpu.VMEM((rows, width), BF16),
            pltpu.VMEM((2, FEAT, rows), BF16),
            pltpu.VMEM((2, rows, FEAT), BF16),
            pltpu.VMEM((rows, width), F32),
            pltpu.VMEM((rows, width), F32),
            pltpu.VMEM((FEAT, width), BF16),
            pltpu.VMEM((nz, SLICE, width), BF16),
            pltpu.VMEM((nz, SLICE, width), F32),
            pltpu.VMEM((nz, SLICE, width), BF16),
            pltpu.VMEM((SLICE, width), BF16),
            pltpu.VMEM((nx, SLICE, width), BF16),
            pltpu.VMEM((FEAT, width), BF16),
            pltpu.VMEM((out_rows * n_head, out_cols), BF16),
            pltpu.VMEM((rows, width), BF16),
            pltpu.VMEM((7, rows, width), BF16),
            pltpu.VMEM((rows, out_cols), F32),
            dma,
            dma((7,)),
            dma((7 * PARTS,)),
            dma((7 * PARTS,)),
            dma((2,)),
            dma((len(OWNER_Z),)),
            dma((nz,)),
            dma((nx,)),
            dma((nx,)),
            dma((nz,)),
            dma((len(OWNER_Z),)),
            dma((n_head,)),
            dma((n_head,)),
            dma,
            dma((7 * PARTS,)),
            dma((7 * PARTS,)),
            pltpu.SemaphoreType.REGULAR((nz // 2 - 1,)),
        ],
        compiler_params=pltpu.CompilerParams(
            collective_id=0, has_side_effects=True, vmem_limit_bytes=48 << 20
        ),
        name="layer",
    )(
        *(
            pltpu.with_memory_space_constraint(value, pltpu.HBM)
            for value in (
                hidden_in,
                proj_weight.T,
                conv_weight,
                norm_gain.reshape(1, width),
                out_weight,
                jnp.asarray(sel, BF16),
                jnp.asarray(coef.T),
                jnp.asarray(coef),
            )
        )
    )


def solution(mesh):
    return jax.shard_map(
        per_device,
        mesh=mesh,
        in_specs=(P("ctx", "head"), P(None, "head"), P(None, "head"), P("head"), P("head", None)),
        out_specs=P("ctx", "head"),
        check_vma=False,
    )
```
